32 devices in a mesh: fsdp: 4 (over y, x), context: 4 (over z), tensor: 2 (over core).
Axes of the slice: x: 2, y: 2, z: 4, core: 2. Of those that a mesh axis runs over, the one named last changes fastest.
Arguments:
- layer_input: bfloat16 [4, 1024, 2048], P('fsdp', 'context'), may hold values from -6 to 6
- prefix: int32 [4], P('fsdp'), may hold values from 102 to 512
- attn_gain: float32 [2048], P(('fsdp', 'context')), may hold values from 0.1 to 1.9
- q_weight: float32 [2048, 2048], P(('fsdp', 'context'), 'tensor'), may hold values from -0.125 to 0.125
- k_weight: float32 [2048, 512], P(('fsdp', 'context'), 'tensor'), may hold values from -0.125 to 0.125
- v_weight: float32 [2048, 512], P(('fsdp', 'context'), 'tensor'), may hold values from -0.125 to 0.125
- output_weight: float32 [2048, 2048], P(('fsdp', 'context'), 'tensor'), may hold values from -0.75 to 0.75
- mlp_gain: float32 [2048], P(('fsdp', 'context')), may hold values from 0.1 to 1.9
- gate_weight: float32 [2048, 8192], P(('fsdp', 'context'), 'tensor'), may hold values from -0.125 to 0.125
- up_weight: float32 [2048, 8192], P(('fsdp', 'context'), 'tensor'), may hold values from -0.125 to 0.125
- down_weight: float32 [2048, 8192], P(('fsdp', 'context'), 'tensor'), may hold values from -0.0625 to 0.0625
- cotangent: bfloat16 [4, 1024, 2048], P('fsdp', 'context'), may hold values from -6 to 6
Outputs:
- layer_output: bfloat16 [4, 1024, 2048], P('fsdp', 'context')
- input_grad: bfloat16 [4, 1024, 2048], P('fsdp', 'context')
- attn_gain_grad: float32 [2048], P(('fsdp', 'context'))
- q_weight_grad: float32 [2048, 2048], P(('fsdp', 'context'), 'tensor')
- k_weight_grad: float32 [2048, 512], P(('fsdp', 'context'), 'tensor')
- v_weight_grad: float32 [2048, 512], P(('fsdp', 'context'), 'tensor')
- o_weight_grad: float32 [2048, 2048], P(('fsdp', 'context'), 'tensor')
- mlp_gain_grad: float32 [2048], P(('fsdp', 'context'))
- gate_weight_grad: float32 [2048, 8192], P(('fsdp', 'context'), 'tensor')
- up_weight_grad: float32 [2048, 8192], P(('fsdp', 'context'), 'tensor')
- down_weight_grad: float32 [2048, 8192], P(('fsdp', 'context'), 'tensor')
The draws below stay inside these ranges and needn't reach their ends.
Inputs may be any that keep to these rules, and one draw needn't show every extreme that they name: prefix counts whole leading tokens of a sequence of 1024.
All inputs are finite; a program needn't handle non-finite values.
Results may differ from the reference program's by a relative error of at most 0.019.
Values may be sent and summed in bfloat16 or wider, within the bound.
No kernel may reach another device: no remote copies, remote signals or barrier semaphores. Data moves between devices by JAX's collectives and lax.ppermute only.
A program may use at most 384 MiB of HBM per device.

```python
import math
from functools import partial
import jax
import jax.numpy as jnp
from jax import lax

D = 2048
HEADS = 32
KV_HEADS = 8
HEAD_DIM = 64
FF = 8192
LEN = 1024
SEQS = 4
HQ = 2048
KVW = 512


def plant(array, stream_key, low, top_value):
    longest = array.shape.index(max(array.shape))
    spots = []
    for shift in (0, 1):
        where = [jax.random.randint(jax.random.fold_in(stream_key, axis), (), 0, length) for axis, length in enumerate(array.shape)]
        where[longest] = (where[longest] + shift) % array.shape[longest]
        spots.append(tuple(where))
    return array.at[spots[0]].set(low).at[spots[1]].set(top_value)


def levels(rng, dims, cuts, smallest, high):
    loudness = 1.0
    for dim, parts in cuts:
        steps = jax.random.uniform(jax.random.fold_in(jax.random.fold_in(rng, 6), dim), (parts,), jnp.float32, smallest / len(cuts), high / len(cuts))
        loudness = loudness * jnp.repeat(jnp.exp(steps), dims[dim] // parts).reshape((-1,) + (1,) * (len(dims) - 1 - dim))
    return loudness


def normal_values(stream_key, shape, deviation, bound, shards=(), kind=jnp.bfloat16):
    loudness = levels(stream_key, shape, shards, -0.22, 0.18) if shards else 1.0
    values = jax.random.normal(stream_key, shape, jnp.float32) * deviation * loudness
    return jnp.minimum(jnp.maximum(values, -bound), bound).astype(kind)


def setup_inputs(seed: int = 0) -> dict:
    splits = jax.random.split(jax.random.key(seed), 13)
    layer_input = normal_values(splits[0], (SEQS, LEN, D), 1.0, 6.0, ((0, 4), (1, 4)))
    prefix = plant(jax.random.randint(splits[1], (SEQS,), LEN // 10, LEN // 2 + 1), jax.random.fold_in(splits[1], 1), LEN // 10, (LEN // 2 + 1) - 1).astype(jnp.int32)
    attn_gain = jnp.clip(1.0 + 0.18 * jax.random.normal(splits[2], (D,), jnp.float32), 0.1, 1.9)
    q_weight = normal_values(splits[3], (D, HQ), D ** -0.5, 0.125, ((0, 16), (1, 2)), jnp.float32)
    k_weight = normal_values(splits[4], (D, KVW), D ** -0.5, 0.125, ((0, 16), (1, 2)), jnp.float32)
    v_weight = normal_values(splits[5], (D, KVW), D ** -0.5, 0.125, ((0, 16), (1, 2)), jnp.float32)
    output_weight = normal_values(splits[6], (D, HQ), (HQ // 32) ** -0.5, 0.75, ((0, 16), (1, 2)), jnp.float32)
    mlp_gain = jnp.clip(1.0 + 0.18 * jax.random.normal(splits[7], (D,), jnp.float32), 0.1, 1.9)
    gate_weight = normal_values(splits[8], (D, FF), D ** -0.5, 0.125, ((0, 16), (1, 2)), jnp.float32)
    up_weight = normal_values(splits[9], (D, FF), D ** -0.5, 0.125, ((0, 16), (1, 2)), jnp.float32)
    down_weight = normal_values(splits[10], (D, FF), FF ** -0.5, 0.0625, ((0, 16), (1, 2)), jnp.float32)
    cotangent = normal_values(splits[11], (SEQS, LEN, D), 1.0, 6.0, ((0, 4), (1, 4)))
    return {"layer_input": layer_input, "prefix": prefix, "attn_gain": attn_gain, "q_weight": q_weight, "k_weight": k_weight, "v_weight": v_weight, "output_weight": output_weight, "mlp_gain": mlp_gain, "gate_weight": gate_weight, "up_weight": up_weight, "down_weight": down_weight, "cotangent": cotangent}


@jax.custom_vjp
def low(v):
    return lax.optimization_barrier(v.astype(jnp.bfloat16)).astype(jnp.float32)

@jax.custom_vjp
def low_back(v):
    return v

def retained_lower(v):
    return (low(v), None)

def low_pass(kept, grad):
    return (grad,)

def back_keep(v):
    return (v, None)

def back_low(kept, grad):
    return (low(grad),)
low.defvjp(retained_lower, low_pass)
low_back.defvjp(back_keep, back_low)
EPS = 1e-05

def rope_tables(length, head_dim):
    half_dim = head_dim // 2
    freq_index = jnp.arange(half_dim, dtype=jnp.float32)
    base_freq = 1.0 / jnp.power(500000.0, 2.0 * freq_index / head_dim)
    wave_len = 2.0 * math.pi / base_freq
    mix_ratio = jnp.clip((8192.0 / wave_len - 1.0) / 3.0, 0.0, 1.0)
    scaled = (1.0 - mix_ratio) * base_freq / 32.0 + mix_ratio * base_freq
    position = jnp.arange(length, dtype=jnp.float32)
    angles = position[:, None] * scaled[None, :]
    angles = jnp.concatenate([angles, angles], axis=1)
    return (jnp.cos(angles), jnp.sin(angles))

def rotate(tensor_in, cos_table, sin_table):
    half_dim = tensor_in.shape[-1] // 2
    turned = jnp.concatenate([-tensor_in[..., half_dim:], tensor_in[..., :half_dim]], axis=-1)
    return tensor_in * cos_table[:, None, :] + turned * sin_table[:, None, :]

def norm_rows(hidden, gain_row):
    inv_rms = lax.rsqrt(lax.optimization_barrier(jnp.mean(hidden * hidden, axis=-1, keepdims=True)) + EPS)
    return low(hidden * inv_rms * gain_row)

def project(left_operand, weight_matrix):
    return jnp.einsum('pvm,mo->pvo', left_operand, weight_matrix, precision=lax.Precision.HIGHEST)

def project_back(left_operand, weight_matrix):
    return jnp.einsum('vzk,qk->vzq', left_operand, weight_matrix, precision=lax.Precision.HIGHEST)

def attend_one(operands):
    query, keys, values, prefix_len = operands
    grouped = query.reshape(LEN, KV_HEADS, HEADS // KV_HEADS, HEAD_DIM)
    logits = jnp.einsum('ikgd,jkd->kgij', grouped, keys, precision=lax.Precision.HIGHEST) * HEAD_DIM ** (-0.5)
    logits = low_back(logits)
    position = jnp.arange(LEN, dtype=jnp.int32)
    allowed = (position[None, :] <= position[:, None]) | (position[None, :] < prefix_len)
    logits = jnp.where(allowed, logits, -1e+30)
    probs = low(jax.nn.softmax(logits, axis=-1))
    mixed_out = jnp.einsum('kgij,jkd->ikgd', probs, values, precision=lax.Precision.HIGHEST)
    return mixed_out.reshape(LEN, HEADS * HEAD_DIM)

def forward(layer_input, attn_gain, q_weight, k_weight, v_weight, output_weight, mlp_gain, gate_weight, up_weight, down_weight, prefix=None):
    cos_table, sin_table = rope_tables(LEN, HEAD_DIM)
    seq_count = layer_input.shape[0]
    normed = norm_rows(layer_input, low(attn_gain))
    query = low_back(project(normed, low(q_weight)))
    key_proj = low_back(project(normed, low(k_weight)))
    values = low(low_back(project(normed, low(v_weight))))
    query = low(rotate(query.reshape(seq_count, LEN, HEADS, HEAD_DIM), cos_table, sin_table))
    key_proj = low(rotate(key_proj.reshape(seq_count, LEN, KV_HEADS, HEAD_DIM), cos_table, sin_table))
    values = values.reshape(seq_count, LEN, KV_HEADS, HEAD_DIM)
    attended = lax.map(jax.checkpoint(attend_one), (query, key_proj, values, prefix))
    attended = low(low_back(attended))
    resid = layer_input + low_back(project_back(attended, low(output_weight)))
    normed_mlp = norm_rows(resid, low(mlp_gain))
    gate_proj = low_back(project(normed_mlp, low(gate_weight)))
    up_projection = low_back(project(normed_mlp, low(up_weight)))
    inner_act = low(jax.nn.silu(gate_proj) * up_projection)
    return resid + low_back(project_back(inner_act, low(down_weight)))

def reference(layer_input, prefix, attn_gain, q_weight, k_weight, v_weight, output_weight, mlp_gain, gate_weight, up_weight, down_weight, cotangent):
    result, pull = jax.vjp(partial(forward, prefix=prefix), layer_input.astype(jnp.float32), attn_gain, q_weight, k_weight, v_weight, output_weight, mlp_gain, gate_weight, up_weight, down_weight)
    grads = pull(cotangent.astype(jnp.float32))
    return (result.astype(jnp.bfloat16), grads[0].astype(jnp.bfloat16), grads[1], grads[2], grads[3], grads[4], grads[5], grads[6], grads[7], grads[8], grads[9])
```

```python
import math

import jax
import jax.numpy as jnp
from jax import lax
from jax.sharding import PartitionSpec as P

HEADS = 32
KV_HEADS = 8
HEAD_DIM = 64
GROUP = HEADS // KV_HEADS
EPS = 1e-05
LOW = jnp.bfloat16
WIDE = jnp.float32


def rope_tables(positions, head_dim):
    half_dim = head_dim // 2
    freq_index = jnp.arange(half_dim, dtype=WIDE)
    base_freq = 1.0 / jnp.power(500000.0, 2.0 * freq_index / head_dim)
    wave_len = 2.0 * math.pi / base_freq
    mix_ratio = jnp.clip((8192.0 / wave_len - 1.0) / 3.0, 0.0, 1.0)
    scaled = (1.0 - mix_ratio) * base_freq / 32.0 + mix_ratio * base_freq
    angles = positions.astype(WIDE)[:, None] * scaled[None, :]
    angles = jnp.concatenate([angles, angles], axis=1)
    return (jnp.cos(angles), jnp.sin(angles))


def rotate(flat_in, cos_table, sin_table):
    shaped = flat_in.reshape(flat_in.shape[0], -1, HEAD_DIM)
    half_dim = HEAD_DIM // 2
    turned = jnp.concatenate([-shaped[..., half_dim:], shaped[..., :half_dim]], axis=-1)
    out = shaped * cos_table[:, None, :] + turned * sin_table[:, None, :]
    return out.reshape(flat_in.shape)


def matmul(left, right):
    return lax.dot_general(left, right, (((1,), (0,)), ((), ())), preferred_element_type=WIDE)


def matmul_t(left, right):
    return lax.dot_general(left, right, (((1,), (1,)), ((), ())), preferred_element_type=WIDE)


def outer(left, right):
    return lax.dot_general(left, right, (((0,), (0,)), ((), ())), preferred_element_type=WIDE)


def inverse_rms(hidden):
    return lax.rsqrt(jnp.mean(hidden * hidden, axis=-1, keepdims=True) + EPS)


def norm_reverse(hidden, inv_rms, gain_row, grad_in):
    weighted = grad_in * gain_row
    scale = jnp.mean(weighted * hidden, axis=-1, keepdims=True)
    return inv_rms * weighted - hidden * (inv_rms * inv_rms * inv_rms) * scale


class Groups:
    def __init__(self, mesh):
        self.n_f = mesh.shape["fsdp"]
        self.n_c = mesh.shape["context"]
        self.c = lax.axis_index("context")
        self.f = lax.axis_index("fsdp")
        self.t = lax.axis_index("tensor")

    def shift(self, block, axis, count, amount):
        return lax.ppermute(block, axis, [(i, (i + amount) % count) for i in range(count)])

    def swap(self, block):
        return lax.ppermute(block, "tensor", [(0, 1), (1, 0)])

    def along(self, blocks, index, count):
        return [lax.select_n(lax.rem(index - j + count, count), *blocks) for j in range(count)] if count > 1 else blocks

    def exchange(self, blocks):
        n = self.n_c
        got = []
        for k in range(n):
            mine = lax.dynamic_index_in_dim(blocks, lax.rem(self.c + k, n), 0, keepdims=False)
            got.append(mine if k == 0 else self.shift(mine, "context", n, k))
        return self.along(got, self.c, n)

    def gather_rows(self, mine):
        n = self.n_c
        steps = [mine] + [self.shift(mine, "context", n, k) for k in range(1, n)]
        near = jnp.concatenate(steps, axis=0)
        return jnp.concatenate([near, self.swap(near)], axis=0)

    def gather_copied(self, own_pair):
        n = self.n_c
        steps = [self.shift(own_pair[0], "context", n, k) for k in range(1, n)]
        near = jnp.concatenate(steps, axis=0)
        return jnp.concatenate([own_pair[0], near, own_pair[1], self.swap(near)], axis=0)

    def scatter_sum(self, near, far):
        n = self.n_c
        rows = near.shape[0] // n
        pair = near.astype(WIDE) + self.swap(far).astype(WIDE)
        total = pair[:rows]
        low = pair.astype(LOW)
        for k in range(1, n):
            got = self.shift(low[k * rows : (k + 1) * rows], "context", n, n - k)
            total = total + got.astype(WIDE)
        return total

    def both_halves(self, mine):
        other = self.swap(mine)
        first = self.t == 0
        return jnp.concatenate([jnp.where(first, mine, other), jnp.where(first, other, mine)], axis=0)


def attention(query, keys, values, allowed):
    rows = query.shape[0]
    kv = keys.shape[1] // HEAD_DIM
    grouped = query.reshape(rows, kv, -1, HEAD_DIM)
    key_heads = keys.reshape(rows, kv, HEAD_DIM)
    value_heads = values.reshape(rows, kv, HEAD_DIM)
    logits = jnp.einsum("ikgd,jkd->kgij", grouped, key_heads, preferred_element_type=WIDE)
    logits = jnp.where(allowed, logits * HEAD_DIM ** (-0.5), -1e30)
    row_max = jnp.max(logits, axis=-1, keepdims=True)
    exp_scores = jnp.exp(logits - row_max)
    row_total = jnp.sum(exp_scores, axis=-1, keepdims=True)
    probs_low = (exp_scores / row_total).astype(LOW)
    mixed = jnp.einsum("kgij,jkd->ikgd", probs_low, value_heads, preferred_element_type=WIDE)
    return mixed.reshape(rows, -1).astype(LOW), row_max + jnp.log(row_total)


def attention_reverse(query, keys, values, allowed, log_total, grad_out):
    rows = query.shape[0]
    kv = keys.shape[1] // HEAD_DIM
    grouped = query.reshape(rows, kv, -1, HEAD_DIM)
    grad_heads = grad_out.reshape(grouped.shape)
    key_heads = keys.reshape(rows, kv, HEAD_DIM)
    value_heads = values.reshape(rows, kv, HEAD_DIM)
    logits = jnp.einsum("ikgd,jkd->kgij", grouped, key_heads, preferred_element_type=WIDE)
    logits = jnp.where(allowed, logits * HEAD_DIM ** (-0.5), -1e30)
    probs = jnp.exp(logits - log_total)
    value_grad = jnp.einsum("kgij,ikgd->jkd", probs.astype(LOW), grad_heads, preferred_element_type=WIDE)
    grad_probs = jnp.einsum("ikgd,jkd->kgij", grad_heads, value_heads, preferred_element_type=WIDE)
    delta = jnp.sum(probs * grad_probs, axis=-1, keepdims=True)
    grad_scores = (probs * (grad_probs - delta)).astype(LOW)
    scale = HEAD_DIM ** (-0.5)
    query_grad = jnp.einsum("kgij,jkd->ikgd", grad_scores, key_heads, preferred_element_type=WIDE) * scale
    key_grad = jnp.einsum("kgij,ikgd->jkd", grad_scores, grouped, preferred_element_type=WIDE) * scale
    return (
        query_grad.reshape(rows, -1),
        key_grad.reshape(rows, -1),
        value_grad.reshape(rows, -1),
    )


def by_dest(weight, count):
    rows, columns = weight.shape
    return weight.astype(LOW).reshape(rows, count, columns // count).transpose(1, 0, 2)


def kv_by_dest(weight, count):
    rows, columns = weight.shape
    heads = columns // HEAD_DIM
    if count <= heads:
        return by_dest(weight, count)
    return jnp.repeat(by_dest(weight, heads), count // heads, axis=0)


def make_layer(mesh):
    def on_device(
        layer_input,
        prefix,
        attn_gain,
        q_weight,
        k_weight,
        v_weight,
        output_weight,
        mlp_gain,
        gate_weight,
        up_weight,
        down_weight,
        cotangent,
    ):
        g = Groups(mesh)
        n_c, n_f = g.n_c, g.n_f
        x_own = layer_input[0]
        cot_own = cotangent[0]
        local, width = x_own.shape
        half = local // 2
        rows = q_weight.shape[0]

        def halves(own):
            return (
                lax.dynamic_slice_in_dim(own, g.t * half, half, 0),
                lax.dynamic_slice_in_dim(own, (1 - g.t) * half, half, 0),
            )

        x_pair = halves(x_own)
        cot_pair = halves(cot_own)
        x_all = g.gather_copied(x_pair)

        gains = jnp.stack([attn_gain, mlp_gain]).astype(LOW)
        gain_steps = [gains] + [g.shift(gains, "context", n_c, k) for k in range(1, n_c)]
        gains_c = jnp.concatenate(g.along(gain_steps, g.c, n_c), axis=1)
        gain_steps = [gains_c] + [g.shift(gains_c, "fsdp", n_f, k) for k in range(1, n_f)]
        gains_all = jnp.concatenate(g.along(gain_steps, g.f, n_f), axis=1).astype(WIDE)
        gain_one, gain_two = gains_all[0:1], gains_all[1:2]

        def gather_weight(blocks):
            mine = jnp.concatenate(g.exchange(blocks), axis=0)
            return lax.all_gather(mine, "fsdp", axis=0, tiled=True)

        q_cols = q_weight.shape[1] // n_c
        kv_blocks = kv_by_dest(k_weight, n_c), kv_by_dest(v_weight, n_c)
        kv_cols = kv_blocks[0].shape[2]
        qkv_full = gather_weight(jnp.concatenate([by_dest(q_weight, n_c), *kv_blocks], axis=2))
        o_full = gather_weight(by_dest(output_weight, n_c))
        gu_full = gather_weight(jnp.concatenate([by_dest(gate_weight, n_c), by_dest(up_weight, n_c)], axis=2))
        down_full = gather_weight(by_dest(down_weight, n_c))
        cot_all = g.gather_copied(cot_pair)

        step = jnp.arange(n_c, dtype=jnp.int32)
        block = lax.rem(g.c - step + n_c, n_c) * local
        side = jnp.stack([g.t, 1 - g.t]).astype(jnp.int32) * half
        positions = (
            side[:, None, None] + block[None, :, None] + jnp.arange(half, dtype=jnp.int32)[None, None, :]
        ).reshape(-1)
        cos_table, sin_table = rope_tables(positions, HEAD_DIM)
        allowed = (positions[None, :] <= positions[:, None]) | (positions[None, :] < prefix[0])

        hidden_in = x_all.astype(WIDE)
        rms_one = inverse_rms(hidden_in)
        normed_one = (hidden_in * rms_one * gain_one).astype(LOW)
        qkv = matmul(normed_one, qkv_full)
        query_rot = rotate(qkv[:, :q_cols], cos_table, sin_table).astype(LOW)
        key_rot = rotate(qkv[:, q_cols : q_cols + kv_cols], cos_table, sin_table).astype(LOW)
        value_low = qkv[:, q_cols + kv_cols :].astype(LOW)
        attended, log_total = attention(query_rot, key_rot, value_low, allowed)

        near_rows = n_c * half
        far_part = matmul_t(attended[near_rows:], o_full).astype(LOW)
        near_part = matmul_t(attended[:near_rows], o_full)
        x_mine = x_pair[0].astype(WIDE)
        resid = x_mine + g.scatter_sum(near_part, far_part)
        rms_two = inverse_rms(resid)
        normed_two = g.gather_rows((resid * rms_two * gain_two).astype(LOW))

        gate_up = matmul(normed_two, gu_full)
        hid = gate_up.shape[1] // 2
        gate_proj, up_proj = gate_up[:, :hid], gate_up[:, hid:]
        squash = jax.nn.sigmoid(gate_proj)
        inner = (gate_proj * squash * up_proj).astype(LOW)
        grad_inner = matmul(cot_all, down_full)
        grad_gate = grad_inner * up_proj * squash * (1.0 + gate_proj * (1.0 - squash))
        grad_up = grad_inner * gate_proj * squash
        grad_gu = jnp.concatenate([grad_gate.astype(LOW), grad_up.astype(LOW)], axis=1)
        far_grad = matmul_t(grad_gu[near_rows:], gu_full).astype(LOW)
        near_grad = matmul_t(grad_gu[:near_rows], gu_full)
        grad_normed_two = g.scatter_sum(near_grad, far_grad)
        cot_mine = cot_pair[0].astype(WIDE)
        grad_resid = cot_mine + norm_reverse(resid, rms_two, gain_two, grad_normed_two)
        branch_all = g.gather_rows(grad_resid.astype(LOW))

        far_out = matmul_t(inner[near_rows:], down_full).astype(LOW)
        near_out = matmul_t(inner[:near_rows], down_full)
        layer_output = g.both_halves((resid + g.scatter_sum(near_out, far_out)).astype(LOW))

        def return_weight(part):
            mine = lax.psum_scatter(part.astype(LOW), "fsdp", scatter_dimension=0, tiled=True)
            return g.exchange(mine.reshape(n_c, rows, part.shape[1]))

        gu_blocks = return_weight(outer(normed_two, grad_gu))
        down_blocks = return_weight(outer(cot_all, inner))

        def cols(blocks, start, size):
            return jnp.concatenate([b[:, start : start + size] for b in blocks], axis=1).astype(WIDE)

        gate_grad = cols(gu_blocks, 0, hid)
        up_grad = cols(gu_blocks, hid, hid)
        down_grad = cols(down_blocks, 0, hid)

        grad_att = matmul(branch_all, o_full).astype(LOW)
        o_blocks = return_weight(outer(branch_all, attended))
        o_grad = cols(o_blocks, 0, q_cols)
        q_grad_rot, k_grad_rot, value_grad = attention_reverse(
            query_rot, key_rot, value_low, allowed, log_total, grad_att
        )
        grad_qkv = jnp.concatenate(
            [
                rotate(q_grad_rot, cos_table, -sin_table).astype(LOW),
                rotate(k_grad_rot, cos_table, -sin_table).astype(LOW),
                value_grad.astype(LOW),
            ],
            axis=1,
        )
        far_one = matmul_t(grad_qkv[near_rows:], qkv_full).astype(LOW)
        near_one = matmul_t(grad_qkv[:near_rows], qkv_full)
        grad_normed_one = g.scatter_sum(near_one, far_one)
        qkv_blocks = return_weight(outer(normed_one, grad_qkv))
        q_grad = cols(qkv_blocks, 0, q_cols)

        def kv_grad(start):
            parts = [b[:, start : start + kv_cols].astype(WIDE) for b in qkv_blocks]
            copies = n_c * kv_cols // k_weight.shape[1]
            return jnp.concatenate([sum(parts[j : j + copies]) for j in range(0, n_c, copies)], axis=1)

        k_grad = kv_grad(q_cols)
        v_grad = kv_grad(q_cols + kv_cols)
        rms_mine = inverse_rms(x_mine)
        grad_in = grad_resid + norm_reverse(x_mine, rms_mine, gain_one, grad_normed_one)
        input_grad = g.both_halves(grad_in.astype(LOW))

        def gain_grad(gain, pairs):
            total = sum(jnp.sum(grad * weight.astype(LOW).astype(WIDE), axis=1) for grad, weight in pairs)
            return (total + g.swap(total)) / gain.astype(LOW).astype(WIDE)

        attn_gain_grad = gain_grad(attn_gain, [(q_grad, q_weight), (k_grad, k_weight), (v_grad, v_weight)])
        mlp_gain_grad = gain_grad(mlp_gain, [(gate_grad, gate_weight), (up_grad, up_weight)])
        return (
            layer_output[None],
            input_grad[None],
            attn_gain_grad,
            q_grad,
            k_grad,
            v_grad,
            o_grad,
            mlp_gain_grad,
            gate_grad,
            up_grad,
            down_grad,
        )

    return on_device


def solution(mesh):
    tokens = P("fsdp", "context", None)
    gain = P(("fsdp", "context"))
    weight = P(("fsdp", "context"), "tensor")
    return jax.shard_map(
        make_layer(mesh),
        mesh=mesh,
        in_specs=(tokens, P("fsdp"), gain, weight, weight, weight, weight, gain, weight, weight, weight, tokens),
        out_specs=(tokens, tokens, gain, weight, weight, weight, weight, gain, weight, weight, weight),
        check_vma=False,
    )
```

```python
import math

import jax
import jax.numpy as jnp
from jax import lax
from jax.experimental import pallas as pl
from jax.experimental.pallas import tpu as pltpu
from jax.sharding import PartitionSpec as P

HEADS = 32
KV_HEADS = 8
HEAD_DIM = 64
GROUP = HEADS // KV_HEADS
EPS = 1e-05
LOW = jnp.bfloat16
WIDE = jnp.float32


def rope_tables(positions, head_dim):
    half_dim = head_dim // 2
    freq_index = jnp.arange(half_dim, dtype=WIDE)
    base_freq = 1.0 / jnp.power(500000.0, 2.0 * freq_index / head_dim)
    wave_len = 2.0 * math.pi / base_freq
    mix_ratio = jnp.clip((8192.0 / wave_len - 1.0) / 3.0, 0.0, 1.0)
    scaled = (1.0 - mix_ratio) * base_freq / 32.0 + mix_ratio * base_freq
    angles = positions.astype(WIDE)[:, None] * scaled[None, :]
    angles = jnp.concatenate([angles, angles], axis=1)
    return (jnp.cos(angles), jnp.sin(angles))


def matmul(left, right):
    return lax.dot_general(left, right, (((1,), (0,)), ((), ())), preferred_element_type=WIDE)


def matmul_t(left, right):
    return lax.dot_general(left, right, (((1,), (1,)), ((), ())), preferred_element_type=WIDE)


def outer(left, right):
    return lax.dot_general(left, right, (((0,), (0,)), ((), ())), preferred_element_type=WIDE)


def inverse_rms(hidden):
    return lax.rsqrt(jnp.mean(hidden * hidden, axis=-1, keepdims=True) + EPS)


def norm_reverse(hidden, inv_rms, gain_row, grad_in):
    weighted = grad_in * gain_row
    scale = jnp.mean(weighted * hidden, axis=-1, keepdims=True)
    return inv_rms * weighted - hidden * (inv_rms * inv_rms * inv_rms) * scale


def after(value, *earlier):
    return lax.optimization_barrier((value, *earlier))[0]


class Groups:
    def __init__(self, mesh):
        self.n_f = mesh.shape["fsdp"]
        self.n_c = mesh.shape["context"]
        self.c = lax.axis_index("context")
        self.t = lax.axis_index("tensor")
        self.bits = [self.n_c >> (i + 1) for i in range(self.n_c.bit_length() - 1)]
        self.order = [0]
        for bit in self.bits:
            self.order = self.order + [o ^ bit for o in self.order]

    def flip(self, block, mask):
        return lax.ppermute(block, "context", [(i, i ^ mask) for i in range(self.n_c)])

    def swap(self, block):
        return lax.ppermute(block, "tensor", [(0, 1), (1, 0)])

    def exchange(self, blocks):
        got = [lax.dynamic_index_in_dim(blocks, self.c ^ mask, 0, keepdims=False) for mask in range(self.n_c)]
        return [self.flip(mine, mask) if mask else mine for mask, mine in enumerate(got)]

    def by_source(self, got):
        return [lax.select_n(self.c ^ j, *got) for j in range(self.n_c)]

    def add_far(self, near, far):
        return near.astype(WIDE) + self.swap(far).astype(WIDE)

    def with_far(self, near):
        return jnp.concatenate([near, self.swap(near)], axis=0)

    def gather_near(self, near):
        for bit in self.bits:
            near = jnp.concatenate([near, self.flip(near, bit)], axis=0)
        return near

    def scatter_step(self, total, bit):
        keep = total.shape[0] // 2
        return total[:keep], self.flip(total[keep:].astype(LOW), bit)

    def scatter_near(self, total):
        for bit in reversed(self.bits):
            kept, got = self.scatter_step(total, bit)
            total = kept + got.astype(WIDE)
        return total

    def scatter_and_gather(self, total, near):
        for low_bit, high_bit in zip(reversed(self.bits), self.bits):
            kept, got = self.scatter_step(total, low_bit)
            there = self.flip(near, high_bit)
            got, there = lax.optimization_barrier((got, there))
            total = kept + got.astype(WIDE)
            near = jnp.concatenate([near, there], axis=0)
        return total, near

    def both_halves(self, mine):
        other = self.swap(mine)
        first = self.t == 0
        return jnp.concatenate([jnp.where(first, mine, other), jnp.where(first, other, mine)], axis=0)


def halves_turned(pair):
    lane = lax.broadcasted_iota(jnp.int32, pair.shape, 1) % HEAD_DIM
    half_dim = HEAD_DIM // 2
    ahead = pltpu.roll(pair, pair.shape[1] - half_dim, 1)
    behind = pltpu.roll(pair, half_dim, 1)
    return jnp.where(lane < half_dim, ahead, behind)


def turn(pair, cos_pair, sin_pair):
    return pair * cos_pair + halves_turned(pair) * sin_pair


def on_lanes(pair, side):
    lane = lax.broadcasted_iota(jnp.int32, pair.shape, 1)
    return jnp.where((lane >= HEAD_DIM) == bool(side), pair, jnp.zeros_like(pair))


def masked(scores, key_pos, limit):
    return jnp.where(key_pos <= limit, scores * HEAD_DIM ** (-0.5), -1e30)


def dot_nt(left, right):
    return lax.dot_general(left, right, (((1,), (1,)), ((), ())), preferred_element_type=WIDE)


def dot_nn(left, right):
    return lax.dot_general(left, right, (((1,), (0,)), ((), ())), preferred_element_type=WIDE)


def dot_tn(left, right):
    return lax.dot_general(left, right, (((0,), (0,)), ((), ())), preferred_element_type=WIDE)


def attention_kernel(
    prefix, limit_ref, key_pos_ref, cos_ref, sin_ref, kv_cos_ref, kv_sin_ref, q_ref, kv_ref,
    q_out, kv_out, mixed_out, log_out, keys, values,
):
    @pl.when(pl.program_id(0) == 0)
    def _():
        kv = turn(kv_ref[...], kv_cos_ref[...], kv_sin_ref[...])
        kv_out[...] = kv.astype(LOW)
        kv = kv.astype(LOW).astype(WIDE)
        first = on_lanes(kv, 0)
        second = on_lanes(kv, 1)
        keys[0] = first.astype(LOW)
        keys[1] = pltpu.roll(first, HEAD_DIM, 1).astype(LOW)
        values[0] = jnp.transpose(pltpu.roll(second, HEAD_DIM, 1)).astype(LOW)
        values[1] = jnp.transpose(second).astype(LOW)

    limit = jnp.maximum(limit_ref[...], prefix[0] - 1)
    key_pos = key_pos_ref[...]
    for pair in range(q_ref.shape[1] // 128):
        lanes = slice(pair * 128, pair * 128 + 128)
        query = turn(q_ref[:, lanes], cos_ref[...], sin_ref[...]).astype(LOW)
        q_out[:, lanes] = query
        mixed = None
        for side in range(2):
            scores = masked(dot_nt(keys[side], query), key_pos, limit)
            top = jnp.max(scores, axis=0, keepdims=True)
            powers = jnp.exp(scores - top)
            total = jnp.sum(powers, axis=0, keepdims=True)
            part = dot_nn(values[side], (powers * (1.0 / total)).astype(LOW))
            mixed = part if mixed is None else mixed + part
            log_out[2 * pair + side : 2 * pair + side + 1, :] = top + jnp.log(total)
        mixed_out[:, lanes] = jnp.transpose(mixed).astype(LOW)


def attention_back_kernel(
    prefix, limit_ref, key_pos_ref, cos_ref, sin_ref, kv_cos_ref, kv_sin_ref, log_ref, q_ref, kv_ref, grad_ref,
    out_ref, keys, values, total,
):
    step = pl.program_id(0)
    width = q_ref.shape[1]
    rows = q_ref.shape[0]

    @pl.when(step == 0)
    def _():
        kv = kv_ref[...].astype(WIDE)
        first = on_lanes(kv, 0)
        second = on_lanes(kv, 1)
        keys[0] = first.astype(LOW)
        keys[1] = pltpu.roll(first, HEAD_DIM, 1).astype(LOW)
        values[0] = pltpu.roll(second, HEAD_DIM, 1).astype(LOW)
        values[1] = second.astype(LOW)
        total[...] = jnp.zeros_like(total)

    limit = jnp.maximum(limit_ref[...], prefix[0] - 1)
    key_pos = key_pos_ref[...]
    for pair in range(width // 128):
        lanes = slice(pair * 128, pair * 128 + 128)
        query = q_ref[:, lanes]
        grad = grad_ref[:, lanes]
        q_grad = None
        for side in range(2):
            head = 2 * pair + side
            scores = masked(dot_nt(keys[side], query), key_pos, limit)
            probs = jnp.exp(scores - log_ref[head : head + 1, :])
            grad_probs = dot_nt(values[side], grad)
            delta = jnp.sum(probs * grad_probs, axis=0, keepdims=True)
            grad_scores = (probs * (grad_probs - delta)).astype(LOW)
            mine = on_lanes(grad.astype(WIDE), side)
            asked = on_lanes(query.astype(WIDE), side)
            mine = mine if side else pltpu.roll(mine, HEAD_DIM, 1)
            asked = pltpu.roll(asked, HEAD_DIM, 1) if side else asked
            total[...] += dot_nn(probs.astype(LOW), mine.astype(LOW)) + dot_nn(grad_scores, asked.astype(LOW))
            part = dot_tn(grad_scores, keys[side])
            q_grad = part if q_grad is None else q_grad + part
        turned = turn(q_grad * HEAD_DIM ** (-0.5), cos_ref[...], -sin_ref[...])
        out_ref[pl.ds(step * rows, rows), lanes] = turned.astype(LOW)

    @pl.when(step == pl.num_programs(0) - 1)
    def _():
        kv = total[...]
        lane = lax.broadcasted_iota(jnp.int32, kv.shape, 1)
        kv = jnp.where(lane < HEAD_DIM, kv * HEAD_DIM ** (-0.5), kv)
        out_ref[:, width:] = turn(kv, kv_cos_ref[...], -kv_sin_ref[...]).astype(LOW)


def attention_specs(tokens, width, rows):
    whole = lambda *shape: pl.BlockSpec(shape, lambda i: (0,) * len(shape))
    per_row = lambda cols: pl.BlockSpec((rows, cols), lambda i: (i, 0))
    shared = [
        pl.BlockSpec(memory_space=pltpu.SMEM),
        pl.BlockSpec((1, rows), lambda i: (0, i)),
        whole(tokens, 1),
        per_row(128),
        per_row(128),
        whole(tokens, 128),
        whole(tokens, 128),
    ]
    return whole, per_row, shared


ROWS = 256


def attention_cost(tokens, width, dots):
    heads = width // HEAD_DIM
    return pl.CostEstimate(
        flops=dots * 2 * heads * tokens * tokens * 128,
        bytes_accessed=tokens * width * 12,
        transcendentals=heads * tokens * tokens,
    )


def attention(qkv, shared):
    tokens = qkv.shape[0]
    width = qkv.shape[1] - 128
    whole, per_row, specs = attention_specs(tokens, width, ROWS)
    return pl.pallas_call(
        attention_kernel,
        grid=(tokens // ROWS,),
        in_specs=specs
        + [per_row(width), pl.BlockSpec((tokens, 128), lambda i: (0, width // 128))],
        out_specs=[per_row(width), whole(tokens, 128), per_row(width), pl.BlockSpec((8, ROWS), lambda i: (0, i))],
        out_shape=[
            jax.ShapeDtypeStruct((tokens, width), LOW),
            jax.ShapeDtypeStruct((tokens, 128), LOW),
            jax.ShapeDtypeStruct((tokens, width), LOW),
            jax.ShapeDtypeStruct((8, tokens), WIDE),
        ],
        scratch_shapes=[pltpu.VMEM((2, tokens, 128), LOW), pltpu.VMEM((2, 128, tokens), LOW)],
        compiler_params=pltpu.CompilerParams(vmem_limit_bytes=40 << 20),
        cost_estimate=attention_cost(tokens, width, 2),
        name="attention",
    )(*shared, qkv, qkv)


def attention_back(query, kv, logs, grad, shared):
    tokens, width = query.shape
    whole, per_row, specs = attention_specs(tokens, width, ROWS)
    return pl.pallas_call(
        attention_back_kernel,
        grid=(tokens // ROWS,),
        in_specs=specs
        + [pl.BlockSpec((8, ROWS), lambda i: (0, i)), per_row(width), whole(tokens, 128), per_row(width)],
        out_specs=whole(tokens, width + 128),
        out_shape=jax.ShapeDtypeStruct((tokens, width + 128), LOW),
        scratch_shapes=[
            pltpu.VMEM((2, tokens, 128), LOW),
            pltpu.VMEM((2, tokens, 128), LOW),
            pltpu.VMEM((tokens, 128), WIDE),
        ],
        compiler_params=pltpu.CompilerParams(vmem_limit_bytes=40 << 20),
        cost_estimate=attention_cost(tokens, width, 5),
        name="attention_back",
    )(*shared, logs, query, kv, grad)


def by_dest(weight, count):
    rows, columns = weight.shape
    return weight.astype(LOW).reshape(rows, count, columns // count).transpose(1, 0, 2)


def kv_by_dest(weight, count):
    rows, columns = weight.shape
    heads = columns // HEAD_DIM
    if count <= heads:
        return by_dest(weight, count)
    return jnp.repeat(by_dest(weight, heads), count // heads, axis=0)


def make_layer(mesh):
    def on_device(
        layer_input,
        prefix,
        attn_gain,
        q_weight,
        k_weight,
        v_weight,
        output_weight,
        mlp_gain,
        gate_weight,
        up_weight,
        down_weight,
        cotangent,
    ):
        g = Groups(mesh)
        n_c = g.n_c
        x_own = layer_input[0]
        local, width = x_own.shape
        half = local // 2
        rows = q_weight.shape[0]

        def join_weight(got):
            return lax.all_gather(jnp.concatenate(g.by_source(got), axis=0), "fsdp", axis=0, tiled=True)

        x_mine = lax.dynamic_slice_in_dim(x_own, g.t * half, half, 0)
        cot_mine = lax.dynamic_slice_in_dim(cotangent[0], g.t * half, half, 0)
        q_cols = q_weight.shape[1] // n_c
        kv_blocks = kv_by_dest(k_weight, n_c), kv_by_dest(v_weight, n_c)
        kv_cols = kv_blocks[0].shape[2]
        wide = q_cols + 2 * kv_cols
        gains = jnp.pad(jnp.stack([attn_gain, mlp_gain], axis=1).astype(LOW), ((0, 0), (0, 126)))
        gain_blocks = jnp.broadcast_to(gains[None], (n_c, *gains.shape))
        attn_got = g.exchange(
            jnp.concatenate(
                [by_dest(q_weight, n_c), *kv_blocks, gain_blocks, by_dest(output_weight, n_c)], axis=2
            )
        )
        x_near = x_mine
        for place, bit in enumerate(g.bits):
            there = g.flip(x_near, bit)
            if place == 0:
                there, *attn_got = lax.optimization_barrier((there, *attn_got))
                gu_got = g.exchange(
                    after(
                        jnp.concatenate([by_dest(gate_weight, n_c), by_dest(up_weight, n_c)], axis=2), there
                    )
                )
            x_near = jnp.concatenate([x_near, there], axis=0)
        attn_full = join_weight(attn_got)
        x_all = g.with_far(x_near)
        gains_all = attn_full[:, wide : wide + 2].T.astype(WIDE)
        qkv_full = attn_full[:, :wide]
        o_full = attn_full[:, wide + 128 :]
        gain_one, gain_two = gains_all[0:1], gains_all[1:2]

        block = (g.c ^ jnp.array(g.order, jnp.int32)) * local
        side = jnp.stack([g.t, 1 - g.t]).astype(jnp.int32) * half
        positions = (
            side[:, None, None] + block[None, :, None] + jnp.arange(half, dtype=jnp.int32)[None, None, :]
        ).reshape(-1)
        cos_table, sin_table = rope_tables(positions, HEAD_DIM)
        half_dim = HEAD_DIM // 2
        sin_table = jnp.concatenate([-sin_table[:, :half_dim], sin_table[:, half_dim:]], axis=1)
        tables = (
            prefix,
            positions[None, :],
            positions[:, None],
            jnp.tile(cos_table, (1, 2)),
            jnp.tile(sin_table, (1, 2)),
            jnp.concatenate([cos_table, jnp.ones_like(cos_table)], axis=1),
            jnp.concatenate([sin_table, jnp.zeros_like(sin_table)], axis=1),
        )

        hidden_in = x_all.astype(WIDE)
        rms_one = inverse_rms(hidden_in)
        normed_one = (hidden_in * rms_one * gain_one).astype(LOW)
        qkv = matmul(normed_one, qkv_full)
        down_got = g.exchange(after(by_dest(down_weight, n_c), qkv))
        query_rot, kv_rot, attended, logs = attention(qkv, tables)
        gu_got, down_got, attended = lax.optimization_barrier((gu_got, down_got, attended))
        gu_full = join_weight(gu_got)
        down_full = join_weight(down_got)
        near_rows = n_c * half
        far_part = matmul_t(attended[near_rows:], o_full).astype(LOW)
        near_part = matmul_t(attended[:near_rows], o_full)
        x_mine = x_mine.astype(WIDE)
        branch, cot_near = g.scatter_and_gather(g.add_far(near_part, far_part), after(cot_mine, attended))
        cot_all = g.with_far(cot_near)
        resid = x_mine + branch
        rms_two = inverse_rms(resid)
        normed_two = g.with_far(g.gather_near((resid * rms_two * gain_two).astype(LOW)))

        gate_up = matmul(normed_two, gu_full)
        hid = gate_up.shape[1] // 2
        gate_proj, up_proj = gate_up[:, :hid], gate_up[:, hid:]
        squash = jax.nn.sigmoid(gate_proj)
        inner = (gate_proj * squash * up_proj).astype(LOW)
        grad_inner = matmul(cot_all, down_full)
        grad_gate = grad_inner * up_proj * squash * (1.0 + gate_proj * (1.0 - squash))
        grad_up = grad_inner * gate_proj * squash
        grad_gu = jnp.concatenate([grad_gate.astype(LOW), grad_up.astype(LOW)], axis=1)
        far_grad = matmul_t(grad_gu[near_rows:], gu_full).astype(LOW)
        near_grad = matmul_t(grad_gu[:near_rows], gu_full)
        gu_part = outer(normed_two, grad_gu).astype(LOW)
        down_part = outer(cot_all, inner).astype(LOW)
        far_out = matmul_t(inner[near_rows:], down_full).astype(LOW)
        near_out = matmul_t(inner[:near_rows], down_full)
        out_total = g.add_far(near_out, far_out)
        grad_normed_two = g.scatter_near(g.add_far(near_grad, far_grad))
        grad_normed_two, _, _, out_total = lax.optimization_barrier(
            (grad_normed_two, gu_part, down_part, out_total)
        )
        grad_resid = cot_mine.astype(WIDE) + norm_reverse(resid, rms_two, gain_two, grad_normed_two)

        def sum_weight(part):
            return lax.psum_scatter(part, "fsdp", scatter_dimension=0, tiled=True)

        def return_weight(mine):
            return g.exchange(mine.reshape(n_c, rows, mine.shape[1]))

        gu_sum = sum_weight(gu_part)
        out_sum, branch_near = g.scatter_and_gather(out_total, grad_resid.astype(LOW))
        branch_all = g.with_far(branch_near)
        branch_all, gu_sum = lax.optimization_barrier((branch_all, gu_sum))
        down_sum = sum_weight(after(down_part, gu_sum))
        layer_output = g.both_halves((resid + out_sum).astype(LOW))
        gu_got = return_weight(gu_sum)

        def cols(blocks, start, size):
            return jnp.concatenate([b[:, start : start + size] for b in blocks], axis=1).astype(WIDE)

        grad_att = matmul(branch_all, o_full).astype(LOW)
        o_part = outer(branch_all, attended).astype(LOW)
        grad_qkv = attention_back(query_rot, kv_rot, logs, grad_att, tables)
        o_sum = sum_weight(after(o_part, down_sum))
        qkv_part = outer(normed_one, grad_qkv).astype(LOW)
        grad_qkv, down_sum, _, *gu_got = lax.optimization_barrier((grad_qkv, down_sum, qkv_part, *gu_got))
        qkv_sum = sum_weight(after(qkv_part, o_sum))
        gu_blocks = g.by_source(gu_got)
        gate_grad = cols(gu_blocks, 0, hid)
        up_grad = cols(gu_blocks, hid, hid)
        down_got = return_weight(down_sum)
        far_one = matmul_t(grad_qkv[near_rows:], qkv_full).astype(LOW)
        near_one = matmul_t(grad_qkv[:near_rows], qkv_full)
        grad_normed_one = g.scatter_near(g.add_far(near_one, far_one))
        grad_normed_one, o_sum, *down_got = lax.optimization_barrier((grad_normed_one, o_sum, *down_got))
        down_grad = cols(g.by_source(down_got), 0, hid)
        o_grad = cols(g.by_source(return_weight(o_sum)), 0, q_cols)
        qkv_blocks = g.by_source(return_weight(qkv_sum))
        q_grad = cols(qkv_blocks, 0, q_cols)

        def kv_grad(start):
            parts = [b[:, start : start + kv_cols].astype(WIDE) for b in qkv_blocks]
            copies = n_c * kv_cols // k_weight.shape[1]
            return jnp.concatenate([sum(parts[j : j + copies]) for j in range(0, n_c, copies)], axis=1)

        k_grad = kv_grad(q_cols)
        v_grad = kv_grad(q_cols + kv_cols)
        rms_mine = inverse_rms(x_mine)
        grad_in = grad_resid + norm_reverse(x_mine, rms_mine, gain_one, grad_normed_one)
        input_grad = g.both_halves(grad_in.astype(LOW))

        def gain_grad(gain, pairs):
            total = sum(jnp.sum(grad * weight.astype(LOW).astype(WIDE), axis=1) for grad, weight in pairs)
            return (total + g.swap(total)) / gain.astype(LOW).astype(WIDE)

        attn_gain_grad = gain_grad(attn_gain, [(q_grad, q_weight), (k_grad, k_weight), (v_grad, v_weight)])
        mlp_gain_grad = gain_grad(mlp_gain, [(gate_grad, gate_weight), (up_grad, up_weight)])
        return (
            layer_output[None],
            input_grad[None],
            attn_gain_grad,
            q_grad,
            k_grad,
            v_grad,
            o_grad,
            mlp_gain_grad,
            gate_grad,
            up_grad,
            down_grad,
        )

    return on_device


def solution(mesh):
    tokens = P("fsdp", "context", None)
    gain = P(("fsdp", "context"))
    weight = P(("fsdp", "context"), "tensor")
    return jax.shard_map(
        make_layer(mesh),
        mesh=mesh,
        in_specs=(tokens, P("fsdp"), gain, weight, weight, weight, weight, gain, weight, weight, weight, tokens),
        out_specs=(tokens, tokens, gain, weight, weight, weight, weight, gain, weight, weight, weight),
        check_vma=False,
    )
```

```python
import math

import jax
import jax.numpy as jnp
from jax import lax
from jax.experimental import pallas as pl
from jax.experimental.pallas import tpu as pltpu
from jax.sharding import PartitionSpec as P

HEADS = 32
KV_HEADS = 8
HEAD_DIM = 64
GROUP = HEADS // KV_HEADS
EPS = 1e-05
LOW = jnp.bfloat16
WIDE = jnp.float32


def rope_tables(positions, head_dim):
    half_dim = head_dim // 2
    freq_index = jnp.arange(half_dim, dtype=WIDE)
    base_freq = 1.0 / jnp.power(500000.0, 2.0 * freq_index / head_dim)
    wave_len = 2.0 * math.pi / base_freq
    mix_ratio = jnp.clip((8192.0 / wave_len - 1.0) / 3.0, 0.0, 1.0)
    scaled = (1.0 - mix_ratio) * base_freq / 32.0 + mix_ratio * base_freq
    angles = positions.astype(WIDE)[:, None] * scaled[None, :]
    angles = jnp.concatenate([angles, angles], axis=1)
    return (jnp.cos(angles), jnp.sin(angles))


def matmul(left, right):
    return lax.dot_general(left, right, (((1,), (0,)), ((), ())), preferred_element_type=WIDE)


def matmul_t(left, right):
    return lax.dot_general(left, right, (((1,), (1,)), ((), ())), preferred_element_type=WIDE)


def outer(left, right):
    return lax.dot_general(left, right, (((0,), (0,)), ((), ())), preferred_element_type=WIDE)


def inverse_rms(hidden):
    return lax.rsqrt(jnp.mean(hidden * hidden, axis=-1, keepdims=True) + EPS)


def norm_reverse(hidden, inv_rms, gain_row, grad_in):
    weighted = grad_in * gain_row
    scale = jnp.mean(weighted * hidden, axis=-1, keepdims=True)
    return inv_rms * weighted - hidden * (inv_rms * inv_rms * inv_rms) * scale


def after(value, *earlier):
    return lax.optimization_barrier((value, *earlier))[0]


class Groups:
    def __init__(self, mesh):
        self.n_f = mesh.shape["fsdp"]
        self.n_c = mesh.shape["context"]
        self.c = lax.axis_index("context")
        self.t = lax.axis_index("tensor")
        self.bits = [self.n_c >> (i + 1) for i in range(self.n_c.bit_length() - 1)]
        self.order = [0]
        for bit in self.bits:
            self.order = self.order + [o ^ bit for o in self.order]

    def flip(self, block, mask):
        return lax.ppermute(block, "context", [(i, i ^ mask) for i in range(self.n_c)])

    def swap(self, block):
        return lax.ppermute(block, "tensor", [(0, 1), (1, 0)])

    def exchange(self, blocks):
        got = [lax.dynamic_index_in_dim(blocks, self.c ^ mask, 0, keepdims=False) for mask in range(self.n_c)]
        return [self.flip(mine, mask) if mask else mine for mask, mine in enumerate(got)]

    def by_source(self, got):
        return [lax.select_n(self.c ^ j, *got) for j in range(self.n_c)]

    def exchange_pieces(self, piece):
        return [piece(mask) if mask == 0 else self.flip(piece(mask), mask) for mask in range(self.n_c)]

    def of_device(self, rows, mask):
        count = rows.shape[0] // (2 * self.n_c)
        place = self.order.index(mask)
        parts = [rows[(h * self.n_c + place) * count :][:count] for h in range(2)]
        return jnp.concatenate(parts, axis=0)

    def with_far(self, near):
        return jnp.concatenate([near, self.swap(near)], axis=0)

    def by_mask(self, near):
        count = near.shape[0] // self.n_c
        blocks = [near[i * count : (i + 1) * count] for i in range(self.n_c)]
        return [blocks[self.order.index(mask)] for mask in range(self.n_c)]

    def gather_step(self, near, place):
        return self.flip(near, self.bits[place])

    def scatter_step(self, send, place):
        return self.flip(send, self.bits[-1 - place])

    def both_halves(self, mine):
        other = self.swap(mine)
        first = self.t == 0
        return jnp.concatenate([jnp.where(first, mine, other), jnp.where(first, other, mine)], axis=0)


def halves_turned(pair):
    lane = lax.broadcasted_iota(jnp.int32, pair.shape, 1) % HEAD_DIM
    half_dim = HEAD_DIM // 2
    ahead = pltpu.roll(pair, pair.shape[1] - half_dim, 1)
    behind = pltpu.roll(pair, half_dim, 1)
    return jnp.where(lane < half_dim, ahead, behind)


def turn(pair, cos_pair, sin_pair):
    return pair * cos_pair + halves_turned(pair) * sin_pair


def on_lanes(pair, side):
    lane = lax.broadcasted_iota(jnp.int32, pair.shape, 1)
    return jnp.where((lane >= HEAD_DIM) == bool(side), pair, jnp.zeros_like(pair))


def masked(scores, key_pos, limit):
    return jnp.where(key_pos <= limit, scores * HEAD_DIM ** (-0.5), -1e30)


def dot_nt(left, right):
    return lax.dot_general(left, right, (((1,), (1,)), ((), ())), preferred_element_type=WIDE)


def dot_nn(left, right):
    return lax.dot_general(left, right, (((1,), (0,)), ((), ())), preferred_element_type=WIDE)


def dot_tn(left, right):
    return lax.dot_general(left, right, (((0,), (0,)), ((), ())), preferred_element_type=WIDE)


def attention_kernel(
    prefix, limit_ref, key_pos_ref, cos_ref, sin_ref, kv_cos_ref, kv_sin_ref, q_ref, kv_ref,
    q_out, kv_out, mixed_out, log_out, keys, values,
):
    @pl.when(pl.program_id(0) == 0)
    def _():
        kv = turn(kv_ref[...], kv_cos_ref[...], kv_sin_ref[...])
        kv_out[...] = kv.astype(LOW)
        kv = kv.astype(LOW).astype(WIDE)
        first = on_lanes(kv, 0)
        second = on_lanes(kv, 1)
        keys[0] = first.astype(LOW)
        keys[1] = pltpu.roll(first, HEAD_DIM, 1).astype(LOW)
        values[0] = jnp.transpose(pltpu.roll(second, HEAD_DIM, 1)).astype(LOW)
        values[1] = jnp.transpose(second).astype(LOW)

    limit = jnp.maximum(limit_ref[...], prefix[0] - 1)
    key_pos = key_pos_ref[...]
    for pair in range(q_ref.shape[1] // 128):
        lanes = slice(pair * 128, pair * 128 + 128)
        query = turn(q_ref[:, lanes], cos_ref[...], sin_ref[...]).astype(LOW)
        q_out[:, lanes] = query
        mixed = None
        for side in range(2):
            scores = masked(dot_nt(keys[side], query), key_pos, limit)
            top = jnp.max(scores, axis=0, keepdims=True)
            powers = jnp.exp(scores - top)
            total = jnp.sum(powers, axis=0, keepdims=True)
            part = dot_nn(values[side], (powers * (1.0 / total)).astype(LOW))
            mixed = part if mixed is None else mixed + part
            log_out[2 * pair + side : 2 * pair + side + 1, :] = top + jnp.log(total)
        mixed_out[:, lanes] = jnp.transpose(mixed).astype(LOW)


def attention_back_kernel(
    prefix, limit_ref, key_pos_ref, cos_ref, sin_ref, kv_cos_ref, kv_sin_ref, log_ref, q_ref, kv_ref, *refs
):
    pieces, (out_ref, keys, values, total, grad_all) = refs[:-5], refs[-5:]
    step = pl.program_id(0)
    width = q_ref.shape[1]
    rows = q_ref.shape[0]

    @pl.when(step == 0)
    def _():
        kv = kv_ref[...].astype(WIDE)
        first = on_lanes(kv, 0)
        second = on_lanes(kv, 1)
        keys[0] = first.astype(LOW)
        keys[1] = pltpu.roll(first, HEAD_DIM, 1).astype(LOW)
        values[0] = pltpu.roll(second, HEAD_DIM, 1).astype(LOW)
        values[1] = second.astype(LOW)
        total[...] = jnp.zeros_like(total)
        half = pieces[0].shape[0] // 2
        for place, piece in enumerate(pieces):
            for side in range(2):
                first = (side * len(pieces) + place) * half
                grad_all[first : first + half, :] = piece[side * half : (side + 1) * half, :]

    limit = jnp.maximum(limit_ref[...], prefix[0] - 1)
    key_pos = key_pos_ref[...]
    for pair in range(width // 128):
        lanes = slice(pair * 128, pair * 128 + 128)
        query = q_ref[:, lanes]
        grad = grad_all[pl.ds(pl.multiple_of(step * rows, rows), rows), lanes]
        q_grad = None
        for side in range(2):
            head = 2 * pair + side
            scores = masked(dot_nt(keys[side], query), key_pos, limit)
            probs = jnp.exp(scores - log_ref[head : head + 1, :])
            grad_probs = dot_nt(values[side], grad)
            delta = jnp.sum(probs * grad_probs, axis=0, keepdims=True)
            grad_scores = (probs * (grad_probs - delta)).astype(LOW)
            mine = on_lanes(grad.astype(WIDE), side)
            asked = on_lanes(query.astype(WIDE), side)
            mine = mine if side else pltpu.roll(mine, HEAD_DIM, 1)
            asked = pltpu.roll(asked, HEAD_DIM, 1) if side else asked
            total[...] += dot_nn(probs.astype(LOW), mine.astype(LOW)) + dot_nn(grad_scores, asked.astype(LOW))
            part = dot_tn(grad_scores, keys[side])
            q_grad = part if q_grad is None else q_grad + part
        turned = turn(q_grad * HEAD_DIM ** (-0.5), cos_ref[...], -sin_ref[...])
        out_ref[pl.ds(step * rows, rows), lanes] = turned.astype(LOW)

    @pl.when(step == pl.num_programs(0) - 1)
    def _():
        kv = total[...]
        lane = lax.broadcasted_iota(jnp.int32, kv.shape, 1)
        kv = jnp.where(lane < HEAD_DIM, kv * HEAD_DIM ** (-0.5), kv)
        out_ref[:, width:] = turn(kv, kv_cos_ref[...], -kv_sin_ref[...]).astype(LOW)


def attention_specs(tokens, width, rows):
    whole = lambda *shape: pl.BlockSpec(shape, lambda i: (0,) * len(shape))
    per_row = lambda cols: pl.BlockSpec((rows, cols), lambda i: (i, 0))
    shared = [
        pl.BlockSpec(memory_space=pltpu.SMEM),
        pl.BlockSpec((1, rows), lambda i: (0, i)),
        whole(tokens, 1),
        per_row(128),
        per_row(128),
        whole(tokens, 128),
        whole(tokens, 128),
    ]
    return whole, per_row, shared


ROWS = 256


def attention_cost(tokens, width, dots):
    heads = width // HEAD_DIM
    return pl.CostEstimate(
        flops=dots * 2 * heads * tokens * tokens * 128,
        bytes_accessed=tokens * width * 12,
        transcendentals=heads * tokens * tokens,
    )


def attention(qkv, shared):
    tokens = qkv.shape[0]
    width = qkv.shape[1] - 128
    whole, per_row, specs = attention_specs(tokens, width, ROWS)
    return pl.pallas_call(
        attention_kernel,
        grid=(tokens // ROWS,),
        in_specs=specs
        + [per_row(width), pl.BlockSpec((tokens, 128), lambda i: (0, width // 128))],
        out_specs=[per_row(width), whole(tokens, 128), per_row(width), pl.BlockSpec((8, ROWS), lambda i: (0, i))],
        out_shape=[
            jax.ShapeDtypeStruct((tokens, width), LOW),
            jax.ShapeDtypeStruct((tokens, 128), LOW),
            jax.ShapeDtypeStruct((tokens, width), LOW),
            jax.ShapeDtypeStruct((8, tokens), WIDE),
        ],
        scratch_shapes=[pltpu.VMEM((2, tokens, 128), LOW), pltpu.VMEM((2, 128, tokens), LOW)],
        compiler_params=pltpu.CompilerParams(vmem_limit_bytes=40 << 20),
        cost_estimate=attention_cost(tokens, width, 2),
        name="attention",
    )(*shared, qkv, qkv)


def attention_back(query, kv, logs, pieces, shared):
    tokens, width = query.shape
    whole, per_row, specs = attention_specs(tokens, width, ROWS)
    return pl.pallas_call(
        attention_back_kernel,
        grid=(tokens // ROWS,),
        in_specs=specs
        + [pl.BlockSpec((8, ROWS), lambda i: (0, i)), per_row(width), whole(tokens, 128)]
        + [whole(*piece.shape) for piece in pieces],
        out_specs=whole(tokens, width + 128),
        out_shape=jax.ShapeDtypeStruct((tokens, width + 128), LOW),
        scratch_shapes=[
            pltpu.VMEM((2, tokens, 128), LOW),
            pltpu.VMEM((2, tokens, 128), LOW),
            pltpu.VMEM((tokens, 128), WIDE),
            pltpu.VMEM((tokens, width), LOW),
        ],
        compiler_params=pltpu.CompilerParams(vmem_limit_bytes=40 << 20),
        cost_estimate=attention_cost(tokens, width, 5),
        name="attention_back",
    )(*shared, logs, query, kv, *pieces)


def feed_forward_kernel(*refs):
    pieces, (cot_ref, gate_ref, up_ref, down_ref, inner_out, grad_out) = refs[:-6], refs[-6:]
    hidden = grad_out.shape[1] // 2
    place_gate = pl.ds(pl.multiple_of(pl.program_id(0) * HID, HID), HID)
    place_up = pl.ds(pl.multiple_of(hidden + pl.program_id(0) * HID, HID), HID)
    for place, piece in enumerate(pieces):
        rows = slice(place * piece.shape[0], (place + 1) * piece.shape[0])
        gate = dot_nn(piece[...], gate_ref[...])
        up = dot_nn(piece[...], up_ref[...])
        grad = dot_nn(cot_ref[rows, :], down_ref[...])
        squash = lax.logistic(gate)
        act = gate * squash
        inner_out[rows, :] = (act * up).astype(LOW)
        grad_out[rows, place_gate] = (grad * up * squash * (1.0 + gate * (1.0 - squash))).astype(LOW)
        grad_out[rows, place_up] = (grad * act).astype(LOW)


HID = 256


def feed_forward(pieces, cot, gu, down):
    tokens, width = cot.shape
    hidden = down.shape[1]
    once = lambda rows: pl.BlockSpec((rows, width), lambda j: (0, 0), pipeline_mode=pl.Buffered(1))
    return pl.pallas_call(
        feed_forward_kernel,
        grid=(hidden // HID,),
        in_specs=[once(piece.shape[0]) for piece in pieces]
        + [
            once(tokens),
            pl.BlockSpec((width, HID), lambda j: (0, j)),
            pl.BlockSpec((width, HID), lambda j: (0, j + hidden // HID)),
            pl.BlockSpec((width, HID), lambda j: (0, j)),
        ],
        out_specs=[
            pl.BlockSpec((tokens, HID), lambda j: (0, j)),
            pl.BlockSpec((tokens, 2 * hidden), lambda j: (0, 0)),
        ],
        out_shape=[
            jax.ShapeDtypeStruct((tokens, hidden), LOW),
            jax.ShapeDtypeStruct((tokens, 2 * hidden), LOW),
        ],
        compiler_params=pltpu.CompilerParams(vmem_limit_bytes=48 << 20),
        cost_estimate=pl.CostEstimate(
            flops=6 * tokens * width * hidden, bytes_accessed=20 << 20, transcendentals=tokens * hidden
        ),
        name="feed_forward",
    )(*pieces, cot, gu, gu, down)


def far_kernel(left, right, out):
    out[...] = dot_nt(left[...], right[...]).astype(LOW)


def near_kernel(left, right, far, keep, send):
    total = dot_nt(left[...], right[...]) + far[...].astype(WIDE)
    keep[...] = total[: keep.shape[0]]
    send[...] = total[keep.shape[0] :].astype(LOW)


def partial_rows(g, left, right, depth):
    rows = left.shape[0] // 2
    width = right.shape[0]
    cols = 256
    grid = (width // cols,)
    right_spec = pl.BlockSpec((cols, depth), lambda j: (j, 0))
    out_spec = lambda count: pl.BlockSpec((count, cols), lambda j: (0, j))
    params = pltpu.CompilerParams(vmem_limit_bytes=32 << 20)
    cost = pl.CostEstimate(flops=2 * rows * width * depth, bytes_accessed=2 * width * depth, transcendentals=0)
    far = pl.pallas_call(
        far_kernel,
        grid=grid,
        in_specs=[pl.BlockSpec((rows, depth), lambda j: (1, 0)), right_spec],
        out_specs=out_spec(rows),
        out_shape=jax.ShapeDtypeStruct((rows, width), LOW),
        compiler_params=params,
        cost_estimate=cost,
        name="far_rows",
    )(left, right)
    return pl.pallas_call(
        near_kernel,
        grid=grid,
        in_specs=[pl.BlockSpec((rows, depth), lambda j: (0, 0)), right_spec, out_spec(rows)],
        out_specs=[out_spec(rows // 2), out_spec(rows // 2)],
        out_shape=[
            jax.ShapeDtypeStruct((rows // 2, width), WIDE),
            jax.ShapeDtypeStruct((rows // 2, width), LOW),
        ],
        compiler_params=params,
        cost_estimate=cost,
        name="near_rows",
    )(left, right, g.swap(far))


def own_kernel(left, right, far, out):
    out[...] = dot_nt(left[...], right[...]) + far[...].astype(WIDE)


def own_rows(g, left, right):
    rows = left.shape[0] // 2
    width, depth = right.shape[0], left.shape[1]
    cols = 512
    grid = (width // cols,)
    left_spec = lambda place: pl.BlockSpec((rows, depth), lambda j: (place, 0))
    right_spec = pl.BlockSpec((cols, depth), lambda j: (j, 0))
    out_spec = pl.BlockSpec((rows, cols), lambda j: (0, j))
    params = pltpu.CompilerParams(vmem_limit_bytes=32 << 20)
    cost = pl.CostEstimate(flops=2 * rows * width * depth, bytes_accessed=2 * width * depth, transcendentals=0)
    far = pl.pallas_call(
        far_kernel,
        grid=grid,
        in_specs=[left_spec(1), right_spec],
        out_specs=out_spec,
        out_shape=jax.ShapeDtypeStruct((rows, width), LOW),
        compiler_params=params,
        cost_estimate=cost,
        name="far_own",
    )(left, right)
    return pl.pallas_call(
        own_kernel,
        grid=grid,
        in_specs=[left_spec(0), right_spec, out_spec],
        out_specs=out_spec,
        out_shape=jax.ShapeDtypeStruct((rows, width), WIDE),
        compiler_params=params,
        cost_estimate=cost,
        name="own_rows",
    )(left, right, g.swap(far))


def by_dest(weight, count):
    rows, columns = weight.shape
    return weight.astype(LOW).reshape(rows, count, columns // count).transpose(1, 0, 2)


def kv_by_dest(weight, count):
    rows, columns = weight.shape
    heads = columns // HEAD_DIM
    if count <= heads:
        return by_dest(weight, count)
    return jnp.repeat(by_dest(weight, heads), count // heads, axis=0)


def make_layer(mesh):
    def on_device(
        layer_input,
        prefix,
        attn_gain,
        q_weight,
        k_weight,
        v_weight,
        output_weight,
        mlp_gain,
        gate_weight,
        up_weight,
        down_weight,
        cotangent,
    ):
        g = Groups(mesh)
        n_c = g.n_c
        x_own = layer_input[0]
        local, width = x_own.shape
        half = local // 2
        rows = q_weight.shape[0]

        def join_weight(got):
            return lax.all_gather(jnp.concatenate(g.by_source(got), axis=0), "fsdp", axis=0, tiled=True)

        def joined(near, there):
            return jnp.concatenate([near, there], axis=0)

        steps = len(g.bits)
        x_mine = lax.dynamic_slice_in_dim(x_own, g.t * half, half, 0)
        cot_mine = lax.dynamic_slice_in_dim(cotangent[0], g.t * half, half, 0)
        q_cols = q_weight.shape[1] // n_c
        kv_blocks = kv_by_dest(k_weight, n_c), kv_by_dest(v_weight, n_c)
        kv_cols = kv_blocks[0].shape[2]
        wide = q_cols + 2 * kv_cols
        gains = jnp.pad(jnp.stack([attn_gain, mlp_gain], axis=1).astype(LOW), ((0, 0), (0, 126)))
        gain_blocks = jnp.broadcast_to(gains[None], (n_c, *gains.shape))
        qkv_got = g.exchange(jnp.concatenate([by_dest(q_weight, n_c), *kv_blocks, gain_blocks], axis=2))
        o_near = output_weight.astype(LOW)
        beside = g.gather_step(o_near, 0)
        beside, qkv_got = lax.optimization_barrier((beside, qkv_got))
        qkv_full = join_weight(qkv_got)
        hid = gate_weight.shape[1] // n_c
        gate_late, up_late = after((gate_weight, up_weight), qkv_got)
        gu_blocks = jnp.concatenate([by_dest(gate_late, n_c), by_dest(up_late, n_c)], axis=2)
        gu_got = g.exchange(gu_blocks)
        for place in range(1, steps):
            o_near = joined(o_near, beside)
            beside = g.gather_step(o_near, place)
        beside, gu_got = lax.optimization_barrier((beside, gu_got))
        o_full = join_weight(g.by_mask(joined(o_near, beside)))
        gu_full = join_weight(gu_got)
        x_near = after(x_mine, beside)
        for place in range(steps):
            there = g.gather_step(x_near, place)
            if place == 0:
                block = after((g.c ^ jnp.array(g.order, jnp.int32)) * local, gu_got)
                side = jnp.stack([g.t, 1 - g.t]).astype(jnp.int32) * half
                positions = (
                    side[:, None, None] + block[None, :, None] + jnp.arange(half, dtype=jnp.int32)[None, None, :]
                ).reshape(-1)
                cos_table, sin_table = rope_tables(positions, HEAD_DIM)
                half_dim = HEAD_DIM // 2
                sin_table = jnp.concatenate([-sin_table[:, :half_dim], sin_table[:, half_dim:]], axis=1)
                tables = (
                    prefix,
                    positions[None, :],
                    positions[:, None],
                    jnp.tile(cos_table, (1, 2)),
                    jnp.tile(sin_table, (1, 2)),
                    jnp.concatenate([cos_table, jnp.ones_like(cos_table)], axis=1),
                    jnp.concatenate([sin_table, jnp.zeros_like(sin_table)], axis=1),
                )
                down_blocks = by_dest(after(down_weight, gu_got), n_c)
                there, tables, down_blocks = lax.optimization_barrier((there, tables, down_blocks))
                down_got = g.exchange(down_blocks)
            if place == steps - 1:
                there, down_got = lax.optimization_barrier((there, down_got))
            x_near = joined(x_near, there)
        down_full = join_weight(down_got)
        cot_near = after(cot_mine, x_near)
        cot_got = g.gather_step(cot_near, 0)
        x_all = g.with_far(x_near)
        gains_all = qkv_full[:, wide : wide + 2].T.astype(WIDE)
        gain_one, gain_two = gains_all[0:1], gains_all[1:2]

        hidden_in = x_all.astype(WIDE)
        rms_one = inverse_rms(hidden_in)
        normed_one = (hidden_in * rms_one * gain_one).astype(LOW)
        qkv = matmul(normed_one, qkv_full[:, :wide])
        query_rot, kv_rot, attended, logs = attention(qkv, tables)
        attended, cot_got = lax.optimization_barrier((attended, cot_got))
        mixed_own = jnp.concatenate(
            g.by_source(g.exchange_pieces(lambda mask: g.of_device(attended, mask))), axis=1
        )
        x_mine = x_mine.astype(WIDE)
        resid = x_mine + own_rows(g, mixed_own, o_full)
        rms_two = inverse_rms(resid)

        def gather_pieces(near, beside=None):
            for place in range(steps - 1):
                there = g.gather_step(near, place)
                if beside is not None:
                    there = beside(there, place)
                near = joined(near, there)
            there = g.gather_step(near, steps - 1)
            if beside is not None:
                there = beside(there, steps - 1)
            return near, there, g.swap(near), g.swap(there)

        state = {"cot": joined(cot_near, cot_got)}

        def with_cot(there, place):
            if place < steps - 1:
                there, beside = lax.optimization_barrier((there, g.gather_step(state["cot"], place + 1)))
                state["cot"] = joined(state["cot"], beside)
            return there

        n2_pieces = gather_pieces((resid * rms_two * gain_two).astype(LOW), with_cot)
        n2_pieces, gu_full = lax.optimization_barrier((n2_pieces, gu_full))
        cot_all = g.with_far(state["cot"])
        normed_two = jnp.concatenate(n2_pieces, axis=0)

        inner, grad_gu = feed_forward(n2_pieces, cot_all, gu_full, down_full)
        keep, send = partial_rows(g, grad_gu, gu_full, 2 * hid)
        gu_part = outer(normed_two, after(grad_gu, send)).astype(LOW)
        for place in range(steps):
            got = g.scatter_step(send, place)
            if place == 0:
                out_keep, out_send = partial_rows(g, after(inner, gu_part), down_full, hid)
                got, out_send = lax.optimization_barrier((got, out_send))
                down_part = outer(cot_all, after(inner, got)).astype(LOW)
            if place == steps - 1:
                got, out_got, _ = lax.optimization_barrier((got, g.scatter_step(out_send, 0), down_part))
            total = keep + got.astype(WIDE)
            keep, send = total[: total.shape[0] // 2], total[total.shape[0] // 2 :].astype(LOW)
        grad_resid = cot_mine.astype(WIDE) + norm_reverse(resid, rms_two, gain_two, total)

        def sum_weight(part):
            return lax.psum_scatter(part, "fsdp", scatter_dimension=0, tiled=True)

        def return_weight(mine):
            return g.exchange(mine.reshape(n_c, rows, mine.shape[1]))

        gu_sum = sum_weight(gu_part)
        down_sum = sum_weight(down_part)
        def cols(blocks, start, size):
            return jnp.concatenate([b[:, start : start + size] for b in blocks], axis=1).astype(WIDE)

        branch_mine = grad_resid.astype(LOW)
        for place in range(1, steps):
            out_total = out_keep + out_got.astype(WIDE)
            cut = out_total.shape[0] // 2
            out_keep, out_got = out_total[:cut], g.scatter_step(out_total[cut:].astype(LOW), place)
        branch_far, out_got = lax.optimization_barrier((g.swap(branch_mine), out_got))
        branch_own = joined(branch_mine, branch_far)
        grad_mixed = matmul(branch_own, o_full).astype(LOW)
        o_part = outer(branch_own, mixed_own).astype(LOW)
        grad_att = g.exchange_pieces(
            lambda mask: lax.dynamic_slice_in_dim(grad_mixed, (g.c ^ mask) * q_cols, q_cols, 1)
        )
        grad_att = [grad_att[mask] for mask in g.order]
        grad_att, _, gu_sum = lax.optimization_barrier((grad_att, o_part, gu_sum))
        o_sum = sum_weight(o_part)
        gu_got = return_weight(gu_sum)
        grad_qkv = attention_back(query_rot, kv_rot, logs, grad_att, tables)
        qkv_part = outer(normed_one, grad_qkv).astype(LOW)
        grad_qkv, gu_got, down_sum, _ = lax.optimization_barrier((grad_qkv, gu_got, down_sum, qkv_part))
        qkv_sum = sum_weight(qkv_part)
        down_got = return_weight(down_sum)
        keep, send = partial_rows(g, grad_qkv, qkv_full, wide)
        for place in range(steps):
            got = g.scatter_step(send, place)
            if place == 0:
                got, down_got, o_sum = lax.optimization_barrier((got, down_got, o_sum))
                o_got = return_weight(o_sum)
            if place == steps - 1:
                got, o_got, qkv_sum = lax.optimization_barrier((got, o_got, qkv_sum))
            total = keep + got.astype(WIDE)
            keep, send = total[: total.shape[0] // 2], total[total.shape[0] // 2 :].astype(LOW)
        out_total = out_keep + out_got.astype(WIDE)
        layer_output = g.both_halves((resid + out_total).astype(LOW))
        grad_normed_one = total

        gu_blocks = g.by_source(gu_got)
        gate_grad = cols(gu_blocks, 0, hid)
        up_grad = cols(gu_blocks, hid, hid)
        down_grad = cols(g.by_source(down_got), 0, hid)
        qkv_blocks = g.by_source(return_weight(qkv_sum))
        q_grad = cols(qkv_blocks, 0, q_cols)
        o_grad = sum(block.astype(WIDE) for block in o_got)

        def kv_grad(start):
            parts = [b[:, start : start + kv_cols].astype(WIDE) for b in qkv_blocks]
            copies = n_c * kv_cols // k_weight.shape[1]
            return jnp.concatenate([sum(parts[j : j + copies]) for j in range(0, n_c, copies)], axis=1)

        k_grad = kv_grad(q_cols)
        v_grad = kv_grad(q_cols + kv_cols)
        rms_mine = inverse_rms(x_mine)
        grad_in = grad_resid + norm_reverse(x_mine, rms_mine, gain_one, grad_normed_one)
        input_grad = g.both_halves(grad_in.astype(LOW))

        def gain_grad(gain, pairs):
            total = sum(jnp.sum(grad * weight.astype(LOW).astype(WIDE), axis=1) for grad, weight in pairs)
            return (total + g.swap(total)) / gain.astype(LOW).astype(WIDE)

        attn_gain_grad = gain_grad(attn_gain, [(q_grad, q_weight), (k_grad, k_weight), (v_grad, v_weight)])
        mlp_gain_grad = gain_grad(mlp_gain, [(gate_grad, gate_weight), (up_grad, up_weight)])
        return (
            layer_output[None],
            input_grad[None],
            attn_gain_grad,
            q_grad,
            k_grad,
            v_grad,
            o_grad,
            mlp_gain_grad,
            gate_grad,
            up_grad,
            down_grad,
        )

    return on_device


def solution(mesh):
    tokens = P("fsdp", "context", None)
    gain = P(("fsdp", "context"))
    weight = P(("fsdp", "context"), "tensor")
    return jax.shard_map(
        make_layer(mesh),
        mesh=mesh,
        in_specs=(tokens, P("fsdp"), gain, weight, weight, weight, weight, gain, weight, weight, weight, tokens),
        out_specs=(tokens, tokens, gain, weight, weight, weight, weight, gain, weight, weight, weight),
        check_vma=False,
    )
```

```python
import math

import jax
import jax.numpy as jnp
from jax import lax
from jax.experimental import pallas as pl
from jax.experimental.pallas import tpu as pltpu
from jax.sharding import PartitionSpec as P

HEADS = 32
KV_HEADS = 8
HEAD_DIM = 64
GROUP = HEADS // KV_HEADS
EPS = 1e-05
LOW = jnp.bfloat16
WIDE = jnp.float32


def rope_tables(positions, head_dim):
    half_dim = head_dim // 2
    freq_index = jnp.arange(half_dim, dtype=WIDE)
    base_freq = 1.0 / jnp.power(500000.0, 2.0 * freq_index / head_dim)
    wave_len = 2.0 * math.pi / base_freq
    mix_ratio = jnp.clip((8192.0 / wave_len - 1.0) / 3.0, 0.0, 1.0)
    scaled = (1.0 - mix_ratio) * base_freq / 32.0 + mix_ratio * base_freq
    angles = positions.astype(WIDE)[:, None] * scaled[None, :]
    angles = jnp.concatenate([angles, angles], axis=1)
    return (jnp.cos(angles), jnp.sin(angles))


def matmul(left, right):
    return lax.dot_general(left, right, (((1,), (0,)), ((), ())), preferred_element_type=WIDE)


def matmul_t(left, right):
    return lax.dot_general(left, right, (((1,), (1,)), ((), ())), preferred_element_type=WIDE)


def outer(left, right):
    return lax.dot_general(left, right, (((0,), (0,)), ((), ())), preferred_element_type=WIDE)


def inverse_rms(hidden):
    return lax.rsqrt(jnp.mean(hidden * hidden, axis=-1, keepdims=True) + EPS)


def norm_reverse(hidden, inv_rms, gain_row, grad_in):
    weighted = grad_in * gain_row
    scale = jnp.mean(weighted * hidden, axis=-1, keepdims=True)
    return inv_rms * weighted - hidden * (inv_rms * inv_rms * inv_rms) * scale


def after(value, *earlier):
    return lax.optimization_barrier((value, *earlier))[0]


class Groups:
    def __init__(self, mesh):
        self.n_f = mesh.shape["fsdp"]
        self.n_c = mesh.shape["context"]
        self.c = lax.axis_index("context")
        self.t = lax.axis_index("tensor")
        self.bits = [self.n_c >> (i + 1) for i in range(self.n_c.bit_length() - 1)]
        self.order = [0]
        for bit in self.bits:
            self.order = self.order + [o ^ bit for o in self.order]

    def flip(self, block, mask, axis="context"):
        return lax.ppermute(block, axis, [(i, i ^ mask) for i in range(lax.axis_size(axis))])

    def fsdp_parts(self, part):
        f = lax.axis_index("fsdp")
        blocks = part.reshape(self.n_f, part.shape[0] // self.n_f, part.shape[1])
        blocks = [lax.dynamic_index_in_dim(blocks, f ^ mask, 0, keepdims=False) for mask in range(self.n_f)]
        cut = blocks[0].shape[0] // 2
        return [{mask: b[:cut] for mask, b in enumerate(blocks)}, {mask: b[cut:] for mask, b in enumerate(blocks)}]

    def fsdp_bits(self, place):
        count = self.n_f.bit_length() - 1
        return (1 << place, self.n_f >> (place + 1)) if count else ()

    def fsdp_send(self, parts, place):
        sent = []
        for part, bit in zip(parts, self.fsdp_bits(place)):
            away = [part[mask].astype(LOW) for mask in sorted(part) if mask & bit]
            sent.append(self.flip(jnp.concatenate(away, axis=0), bit, "fsdp"))
        return sent

    def fsdp_add(self, parts, sent, place):
        out = []
        for part, got, bit in zip(parts, sent, self.fsdp_bits(place)):
            kept = [mask for mask in sorted(part) if not mask & bit]
            count = got.shape[0] // len(kept)
            order = sorted(mask | bit for mask in kept)
            out.append(
                {
                    mask: part[mask].astype(WIDE) + got[order.index(mask | bit) * count :][:count].astype(WIDE)
                    for mask in kept
                }
            )
        return out

    def swap(self, block):
        return lax.ppermute(block, "tensor", [(0, 1), (1, 0)])

    def exchange(self, blocks):
        got = [lax.dynamic_index_in_dim(blocks, self.c ^ mask, 0, keepdims=False) for mask in range(self.n_c)]
        return [self.flip(mine, mask) if mask else mine for mask, mine in enumerate(got)]

    def by_source(self, got):
        return [lax.select_n(self.c ^ j, *got) for j in range(self.n_c)]

    def exchange_pieces(self, piece):
        return [piece(mask) if mask == 0 else self.flip(piece(mask), mask) for mask in range(self.n_c)]

    def of_device(self, rows, mask):
        count = rows.shape[0] // (2 * self.n_c)
        place = self.order.index(mask)
        parts = [rows[(h * self.n_c + place) * count :][:count] for h in range(2)]
        return jnp.concatenate(parts, axis=0)

    def with_far(self, near):
        return jnp.concatenate([near, self.swap(near)], axis=0)

    def by_mask(self, near):
        count = near.shape[0] // self.n_c
        blocks = [near[i * count : (i + 1) * count] for i in range(self.n_c)]
        return [blocks[self.order.index(mask)] for mask in range(self.n_c)]

    def gather_step(self, near, place):
        return self.flip(near, self.bits[place])

    def scatter_step(self, send, place):
        return self.flip(send, self.bits[-1 - place])

    def both_halves(self, mine):
        other = self.swap(mine)
        first = self.t == 0
        return jnp.concatenate([jnp.where(first, mine, other), jnp.where(first, other, mine)], axis=0)


def halves_turned(pair):
    lane = lax.broadcasted_iota(jnp.int32, pair.shape, 1) % HEAD_DIM
    half_dim = HEAD_DIM // 2
    ahead = pltpu.roll(pair, pair.shape[1] - half_dim, 1)
    behind = pltpu.roll(pair, half_dim, 1)
    return jnp.where(lane < half_dim, ahead, behind)


def turn(pair, cos_pair, sin_pair):
    return pair * cos_pair + halves_turned(pair) * sin_pair


def on_lanes(pair, side):
    lane = lax.broadcasted_iota(jnp.int32, pair.shape, 1)
    return jnp.where((lane >= HEAD_DIM) == bool(side), pair, jnp.zeros_like(pair))


def masked(scores, key_pos, limit):
    return jnp.where(key_pos <= limit, scores * HEAD_DIM ** (-0.5), -1e30)


def dot_nt(left, right):
    return lax.dot_general(left, right, (((1,), (1,)), ((), ())), preferred_element_type=WIDE)


def dot_nn(left, right):
    return lax.dot_general(left, right, (((1,), (0,)), ((), ())), preferred_element_type=WIDE)


def dot_tn(left, right):
    return lax.dot_general(left, right, (((0,), (0,)), ((), ())), preferred_element_type=WIDE)


def attention_kernel(
    prefix, limit_ref, key_pos_ref, cos_ref, sin_ref, kv_cos_ref, kv_sin_ref, q_ref, kv_ref,
    q_out, kv_out, mixed_out, log_out, keys, values,
):
    @pl.when(pl.program_id(0) == 0)
    def _():
        kv = turn(kv_ref[...], kv_cos_ref[...], kv_sin_ref[...])
        kv_out[...] = kv.astype(LOW)
        kv = kv.astype(LOW).astype(WIDE)
        first = on_lanes(kv, 0)
        second = on_lanes(kv, 1)
        keys[0] = first.astype(LOW)
        keys[1] = pltpu.roll(first, HEAD_DIM, 1).astype(LOW)
        values[0] = jnp.transpose(pltpu.roll(second, HEAD_DIM, 1)).astype(LOW)
        values[1] = jnp.transpose(second).astype(LOW)

    limit = jnp.maximum(limit_ref[...], prefix[0] - 1)
    key_pos = key_pos_ref[...]
    for pair in range(q_ref.shape[1] // 128):
        lanes = slice(pair * 128, pair * 128 + 128)
        query = turn(q_ref[:, lanes], cos_ref[...], sin_ref[...]).astype(LOW)
        q_out[:, lanes] = query
        mixed = None
        for side in range(2):
            scores = masked(dot_nt(keys[side], query), key_pos, limit)
            top = jnp.max(scores, axis=0, keepdims=True)
            powers = jnp.exp(scores - top)
            total = jnp.sum(powers, axis=0, keepdims=True)
            part = dot_nn(values[side], (powers * (1.0 / total)).astype(LOW))
            mixed = part if mixed is None else mixed + part
            log_out[2 * pair + side : 2 * pair + side + 1, :] = top + jnp.log(total)
        mixed_out[:, lanes] = jnp.transpose(mixed).astype(LOW)


def attention_back_kernel(
    prefix, limit_ref, key_pos_ref, cos_ref, sin_ref, kv_cos_ref, kv_sin_ref, log_ref, q_ref, kv_ref, *refs
):
    pieces, (out_ref, keys, values, total, grad_all) = refs[:-5], refs[-5:]
    step = pl.program_id(0)
    width = q_ref.shape[1]
    rows = q_ref.shape[0]

    @pl.when(step == 0)
    def _():
        kv = kv_ref[...].astype(WIDE)
        first = on_lanes(kv, 0)
        second = on_lanes(kv, 1)
        keys[0] = first.astype(LOW)
        keys[1] = pltpu.roll(first, HEAD_DIM, 1).astype(LOW)
        values[0] = pltpu.roll(second, HEAD_DIM, 1).astype(LOW)
        values[1] = second.astype(LOW)
        total[...] = jnp.zeros_like(total)
        half = pieces[0].shape[0] // 2
        for place, piece in enumerate(pieces):
            for side in range(2):
                first = (side * len(pieces) + place) * half
                grad_all[first : first + half, :] = piece[side * half : (side + 1) * half, :]

    limit = jnp.maximum(limit_ref[...], prefix[0] - 1)
    key_pos = key_pos_ref[...]
    for pair in range(width // 128):
        lanes = slice(pair * 128, pair * 128 + 128)
        query = q_ref[:, lanes]
        grad = grad_all[pl.ds(pl.multiple_of(step * rows, rows), rows), lanes]
        q_grad = None
        for side in range(2):
            head = 2 * pair + side
            scores = masked(dot_nt(keys[side], query), key_pos, limit)
            probs = jnp.exp(scores - log_ref[head : head + 1, :])
            grad_probs = dot_nt(values[side], grad)
            delta = jnp.sum(probs * grad_probs, axis=0, keepdims=True)
            grad_scores = (probs * (grad_probs - delta)).astype(LOW)
            mine = on_lanes(grad.astype(WIDE), side)
            asked = on_lanes(query.astype(WIDE), side)
            mine = mine if side else pltpu.roll(mine, HEAD_DIM, 1)
            asked = pltpu.roll(asked, HEAD_DIM, 1) if side else asked
            total[...] += dot_nn(probs.astype(LOW), mine.astype(LOW)) + dot_nn(grad_scores, asked.astype(LOW))
            part = dot_tn(grad_scores, keys[side])
            q_grad = part if q_grad is None else q_grad + part
        turned = turn(q_grad * HEAD_DIM ** (-0.5), cos_ref[...], -sin_ref[...])
        out_ref[pl.ds(step * rows, rows), lanes] = turned.astype(LOW)

    @pl.when(step == pl.num_programs(0) - 1)
    def _():
        kv = total[...]
        lane = lax.broadcasted_iota(jnp.int32, kv.shape, 1)
        kv = jnp.where(lane < HEAD_DIM, kv * HEAD_DIM ** (-0.5), kv)
        out_ref[:, width:] = turn(kv, kv_cos_ref[...], -kv_sin_ref[...]).astype(LOW)


def attention_specs(tokens, width, rows):
    whole = lambda *shape: pl.BlockSpec(shape, lambda i: (0,) * len(shape))
    per_row = lambda cols: pl.BlockSpec((rows, cols), lambda i: (i, 0))
    shared = [
        pl.BlockSpec(memory_space=pltpu.SMEM),
        pl.BlockSpec((1, rows), lambda i: (0, i)),
        whole(tokens, 1),
        per_row(128),
        per_row(128),
        whole(tokens, 128),
        whole(tokens, 128),
    ]
    return whole, per_row, shared


ROWS = 256


def attention_cost(tokens, width, dots):
    heads = width // HEAD_DIM
    return pl.CostEstimate(
        flops=dots * 2 * heads * tokens * tokens * 128,
        bytes_accessed=tokens * width * 12,
        transcendentals=heads * tokens * tokens,
    )


def attention(qkv, shared):
    tokens = qkv.shape[0]
    width = qkv.shape[1] - 128
    whole, per_row, specs = attention_specs(tokens, width, ROWS)
    return pl.pallas_call(
        attention_kernel,
        grid=(tokens // ROWS,),
        in_specs=specs
        + [per_row(width), pl.BlockSpec((tokens, 128), lambda i: (0, width // 128))],
        out_specs=[per_row(width), whole(tokens, 128), per_row(width), pl.BlockSpec((8, ROWS), lambda i: (0, i))],
        out_shape=[
            jax.ShapeDtypeStruct((tokens, width), LOW),
            jax.ShapeDtypeStruct((tokens, 128), LOW),
            jax.ShapeDtypeStruct((tokens, width), LOW),
            jax.ShapeDtypeStruct((8, tokens), WIDE),
        ],
        scratch_shapes=[pltpu.VMEM((2, tokens, 128), LOW), pltpu.VMEM((2, 128, tokens), LOW)],
        compiler_params=pltpu.CompilerParams(vmem_limit_bytes=40 << 20),
        cost_estimate=attention_cost(tokens, width, 2),
        name="attention",
    )(*shared, qkv, qkv)


def attention_back(query, kv, logs, pieces, shared):
    tokens, width = query.shape
    whole, per_row, specs = attention_specs(tokens, width, ROWS)
    return pl.pallas_call(
        attention_back_kernel,
        grid=(tokens // ROWS,),
        in_specs=specs
        + [pl.BlockSpec((8, ROWS), lambda i: (0, i)), per_row(width), whole(tokens, 128)]
        + [whole(*piece.shape) for piece in pieces],
        out_specs=whole(tokens, width + 128),
        out_shape=jax.ShapeDtypeStruct((tokens, width + 128), LOW),
        scratch_shapes=[
            pltpu.VMEM((2, tokens, 128), LOW),
            pltpu.VMEM((2, tokens, 128), LOW),
            pltpu.VMEM((tokens, 128), WIDE),
            pltpu.VMEM((tokens, width), LOW),
        ],
        compiler_params=pltpu.CompilerParams(vmem_limit_bytes=40 << 20),
        cost_estimate=attention_cost(tokens, width, 5),
        name="attention_back",
    )(*shared, logs, query, kv, *pieces)


def feed_forward_kernel(*refs):
    pieces, (cot_ref, gate_ref, up_ref, down_ref, inner_out, grad_out) = refs[:-6], refs[-6:]
    hidden = grad_out.shape[1] // 2
    place_gate = pl.ds(pl.multiple_of(pl.program_id(0) * HID, HID), HID)
    place_up = pl.ds(pl.multiple_of(hidden + pl.program_id(0) * HID, HID), HID)
    for place, piece in enumerate(pieces):
        rows = slice(place * piece.shape[0], (place + 1) * piece.shape[0])
        gate = dot_nn(piece[...], gate_ref[...])
        up = dot_nn(piece[...], up_ref[...])
        grad = dot_nn(cot_ref[rows, :], down_ref[...])
        squash = lax.logistic(gate)
        act = gate * squash
        inner_out[rows, :] = (act * up).astype(LOW)
        grad_out[rows, place_gate] = (grad * up * squash * (1.0 + gate * (1.0 - squash))).astype(LOW)
        grad_out[rows, place_up] = (grad * act).astype(LOW)


HID = 256


def feed_forward(pieces, cot, gu, down):
    tokens, width = cot.shape
    hidden = down.shape[1]
    once = lambda rows: pl.BlockSpec((rows, width), lambda j: (0, 0), pipeline_mode=pl.Buffered(1))
    return pl.pallas_call(
        feed_forward_kernel,
        grid=(hidden // HID,),
        in_specs=[once(piece.shape[0]) for piece in pieces]
        + [
            once(tokens),
            pl.BlockSpec((width, HID), lambda j: (0, j)),
            pl.BlockSpec((width, HID), lambda j: (0, j + hidden // HID)),
            pl.BlockSpec((width, HID), lambda j: (0, j)),
        ],
        out_specs=[
            pl.BlockSpec((tokens, HID), lambda j: (0, j)),
            pl.BlockSpec((tokens, 2 * hidden), lambda j: (0, 0)),
        ],
        out_shape=[
            jax.ShapeDtypeStruct((tokens, hidden), LOW),
            jax.ShapeDtypeStruct((tokens, 2 * hidden), LOW),
        ],
        compiler_params=pltpu.CompilerParams(vmem_limit_bytes=48 << 20),
        cost_estimate=pl.CostEstimate(
            flops=6 * tokens * width * hidden, bytes_accessed=20 << 20, transcendentals=tokens * hidden
        ),
        name="feed_forward",
    )(*pieces, cot, gu, gu, down)


def far_kernel(left, right, out):
    out[...] = dot_nt(left[...], right[...]).astype(LOW)


def near_kernel(left, right, far, keep, send):
    total = dot_nt(left[...], right[...]) + far[...].astype(WIDE)
    keep[...] = total[: keep.shape[0]]
    send[...] = total[keep.shape[0] :].astype(LOW)


def partial_rows(g, left, right, depth):
    rows = left.shape[0] // 2
    width = right.shape[0]
    cols = 256
    grid = (width // cols,)
    right_spec = pl.BlockSpec((cols, depth), lambda j: (j, 0))
    out_spec = lambda count: pl.BlockSpec((count, cols), lambda j: (0, j))
    params = pltpu.CompilerParams(vmem_limit_bytes=32 << 20)
    cost = pl.CostEstimate(flops=2 * rows * width * depth, bytes_accessed=2 * width * depth, transcendentals=0)
    far = pl.pallas_call(
        far_kernel,
        grid=grid,
        in_specs=[pl.BlockSpec((rows, depth), lambda j: (1, 0)), right_spec],
        out_specs=out_spec(rows),
        out_shape=jax.ShapeDtypeStruct((rows, width), LOW),
        compiler_params=params,
        cost_estimate=cost,
        name="far_rows",
    )(left, right)
    return pl.pallas_call(
        near_kernel,
        grid=grid,
        in_specs=[pl.BlockSpec((rows, depth), lambda j: (0, 0)), right_spec, out_spec(rows)],
        out_specs=[out_spec(rows // 2), out_spec(rows // 2)],
        out_shape=[
            jax.ShapeDtypeStruct((rows // 2, width), WIDE),
            jax.ShapeDtypeStruct((rows // 2, width), LOW),
        ],
        compiler_params=params,
        cost_estimate=cost,
        name="near_rows",
    )(left, right, g.swap(far))


def own_kernel(left, right, far, out):
    out[...] = dot_nt(left[...], right[...]) + far[...].astype(WIDE)


def own_rows(g, left, right):
    rows = left.shape[0] // 2
    width, depth = right.shape[0], left.shape[1]
    cols = 512
    grid = (width // cols,)
    left_spec = lambda place: pl.BlockSpec((rows, depth), lambda j: (place, 0))
    right_spec = pl.BlockSpec((cols, depth), lambda j: (j, 0))
    out_spec = pl.BlockSpec((rows, cols), lambda j: (0, j))
    params = pltpu.CompilerParams(vmem_limit_bytes=32 << 20)
    cost = pl.CostEstimate(flops=2 * rows * width * depth, bytes_accessed=2 * width * depth, transcendentals=0)
    far = pl.pallas_call(
        far_kernel,
        grid=grid,
        in_specs=[left_spec(1), right_spec],
        out_specs=out_spec,
        out_shape=jax.ShapeDtypeStruct((rows, width), LOW),
        compiler_params=params,
        cost_estimate=cost,
        name="far_own",
    )(left, right)
    return pl.pallas_call(
        own_kernel,
        grid=grid,
        in_specs=[left_spec(0), right_spec, out_spec],
        out_specs=out_spec,
        out_shape=jax.ShapeDtypeStruct((rows, width), WIDE),
        compiler_params=params,
        cost_estimate=cost,
        name="own_rows",
    )(left, right, g.swap(far))


def by_dest(weight, count):
    rows, columns = weight.shape
    return weight.astype(LOW).reshape(rows, count, columns // count).transpose(1, 0, 2)


def kv_by_dest(weight, count):
    rows, columns = weight.shape
    heads = columns // HEAD_DIM
    if count <= heads:
        return by_dest(weight, count)
    return jnp.repeat(by_dest(weight, heads), count // heads, axis=0)


def make_layer(mesh):
    def on_device(
        layer_input,
        prefix,
        attn_gain,
        q_weight,
        k_weight,
        v_weight,
        output_weight,
        mlp_gain,
        gate_weight,
        up_weight,
        down_weight,
        cotangent,
    ):
        g = Groups(mesh)
        n_c = g.n_c
        x_own = layer_input[0]
        local, width = x_own.shape
        half = local // 2
        rows = q_weight.shape[0]

        def join_weight(got):
            return lax.all_gather(jnp.concatenate(g.by_source(got), axis=0), "fsdp", axis=0, tiled=True)

        def joined(near, there):
            return jnp.concatenate([near, there], axis=0)

        steps = len(g.bits)
        x_mine = lax.dynamic_slice_in_dim(x_own, g.t * half, half, 0)
        cot_mine = lax.dynamic_slice_in_dim(cotangent[0], g.t * half, half, 0)
        q_cols = q_weight.shape[1] // n_c
        kv_blocks = kv_by_dest(k_weight, n_c), kv_by_dest(v_weight, n_c)
        kv_cols = kv_blocks[0].shape[2]
        wide = q_cols + 2 * kv_cols
        gains = jnp.pad(jnp.stack([attn_gain, mlp_gain], axis=1).astype(LOW), ((0, 0), (0, 126)))
        gain_blocks = jnp.broadcast_to(gains[None], (n_c, *gains.shape))
        qkv_blocks = jnp.concatenate([by_dest(q_weight, n_c), *kv_blocks], axis=2)
        qkv_rows = qkv_blocks.transpose(1, 0, 2).reshape(rows, n_c * wide)
        qkv_got = g.exchange(jnp.concatenate([qkv_blocks, gain_blocks], axis=2))
        o_near = output_weight.astype(LOW)
        beside = g.gather_step(o_near, 0)
        beside, qkv_got = lax.optimization_barrier((beside, qkv_got))
        qkv_full = join_weight(qkv_got)
        hid = gate_weight.shape[1] // n_c
        gate_late, up_late = after((gate_weight, up_weight), qkv_got)
        gu_blocks = jnp.concatenate([by_dest(gate_late, n_c), by_dest(up_late, n_c)], axis=2)
        gu_got = g.exchange(gu_blocks)
        for place in range(1, steps):
            o_near = joined(o_near, beside)
            beside = g.gather_step(o_near, place)
        beside, gu_got = lax.optimization_barrier((beside, gu_got))
        o_full = join_weight(g.by_mask(joined(o_near, beside)))
        gu_full = join_weight(gu_got)
        x_near = after(x_mine, beside)
        for place in range(steps):
            there = g.gather_step(x_near, place)
            if place == 0:
                block = after((g.c ^ jnp.array(g.order, jnp.int32)) * local, gu_got)
                side = jnp.stack([g.t, 1 - g.t]).astype(jnp.int32) * half
                positions = (
                    side[:, None, None] + block[None, :, None] + jnp.arange(half, dtype=jnp.int32)[None, None, :]
                ).reshape(-1)
                cos_table, sin_table = rope_tables(positions, HEAD_DIM)
                half_dim = HEAD_DIM // 2
                sin_table = jnp.concatenate([-sin_table[:, :half_dim], sin_table[:, half_dim:]], axis=1)
                tables = (
                    prefix,
                    positions[None, :],
                    positions[:, None],
                    jnp.tile(cos_table, (1, 2)),
                    jnp.tile(sin_table, (1, 2)),
                    jnp.concatenate([cos_table, jnp.ones_like(cos_table)], axis=1),
                    jnp.concatenate([sin_table, jnp.zeros_like(sin_table)], axis=1),
                )
                down_blocks = by_dest(after(down_weight, gu_got), n_c)
                there, tables, down_blocks = lax.optimization_barrier((there, tables, down_blocks))
                down_got = g.exchange(down_blocks)
                qkv_rows = after(qkv_rows, there)
                back_got = g.gather_step(qkv_rows, 0)
            if place == steps - 1:
                there, down_got, back_got = lax.optimization_barrier((there, down_got, back_got))
            x_near = joined(x_near, there)
        down_full = join_weight(down_got)
        cot_near = after(cot_mine, x_near)
        cot_got = g.gather_step(cot_near, 0)
        back_near = after(joined(qkv_rows, back_got), x_near)
        for place in range(1, steps):
            back_got = g.gather_step(back_near, place)
            if place < steps - 1:
                back_near = joined(back_near, back_got)
        x_all = g.with_far(x_near)
        gains_all = qkv_full[:, wide : wide + 2].T.astype(WIDE)
        gain_one, gain_two = gains_all[0:1], gains_all[1:2]

        hidden_in = x_all.astype(WIDE)
        rms_one = inverse_rms(hidden_in)
        normed_one = (hidden_in * rms_one * gain_one).astype(LOW)
        qkv = matmul(normed_one, qkv_full[:, :wide])
        query_rot, kv_rot, attended, logs = attention(qkv, tables)
        attended, cot_got, back_got = lax.optimization_barrier((attended, cot_got, back_got))
        mixed_own = jnp.concatenate(
            g.by_source(g.exchange_pieces(lambda mask: g.of_device(attended, mask))), axis=1
        )
        x_mine = x_mine.astype(WIDE)
        resid = x_mine + own_rows(g, mixed_own, o_full)
        rms_two = inverse_rms(resid)

        def gather_pieces(near, beside=None):
            for place in range(steps - 1):
                there = g.gather_step(near, place)
                if beside is not None:
                    there = beside(there, place)
                near = joined(near, there)
            there = g.gather_step(near, steps - 1)
            if beside is not None:
                there = beside(there, steps - 1)
            return near, there, g.swap(near), g.swap(there)

        state = {"cot": joined(cot_near, cot_got), "back": joined(back_near, back_got)}

        def with_cot(there, place):
            if place < steps - 1:
                there, beside = lax.optimization_barrier((there, g.gather_step(state["cot"], place + 1)))
                state["cot"] = joined(state["cot"], beside)
            return there

        n2_pieces = gather_pieces((resid * rms_two * gain_two).astype(LOW), with_cot)
        back_near = state["back"]
        n2_pieces, gu_full = lax.optimization_barrier((n2_pieces, gu_full))
        cot_all = g.with_far(state["cot"])
        normed_two = jnp.concatenate(n2_pieces, axis=0)

        back_full = join_weight(g.by_mask(back_near))
        inner, grad_gu = feed_forward(n2_pieces, cot_all, gu_full, down_full)
        keep, send = partial_rows(g, grad_gu, gu_full, 2 * hid)
        gu_part = outer(normed_two, after(grad_gu, send)).astype(LOW)
        for place in range(steps):
            got = g.scatter_step(send, place)
            if place == 0:
                out_keep, out_send = partial_rows(g, after(inner, gu_part), down_full, hid)
                got, out_send, back_full = lax.optimization_barrier((got, out_send, back_full))
                down_part = outer(cot_all, after(inner, got)).astype(LOW)
            if place == steps - 1:
                got, out_got, _ = lax.optimization_barrier((got, g.scatter_step(out_send, 0), down_part))
            total = keep + got.astype(WIDE)
            keep, send = total[: total.shape[0] // 2], total[total.shape[0] // 2 :].astype(LOW)
        grad_resid = cot_mine.astype(WIDE) + norm_reverse(resid, rms_two, gain_two, total)

        def sum_weight(part):
            return lax.psum_scatter(part, "fsdp", scatter_dimension=0, tiled=True)

        def return_weight(mine):
            return g.exchange(mine.reshape(n_c, rows, mine.shape[1]))

        gu_sum = sum_weight(gu_part)
        down_sums = g.fsdp_parts(down_part)
        stages = g.n_f.bit_length() - 1
        def cols(blocks, start, size):
            return jnp.concatenate([b[:, start : start + size] for b in blocks], axis=1).astype(WIDE)

        branch_mine = grad_resid.astype(LOW)
        for place in range(1, steps):
            out_total = out_keep + out_got.astype(WIDE)
            cut = out_total.shape[0] // 2
            out_keep, out_got = out_total[:cut], g.scatter_step(out_total[cut:].astype(LOW), place)
        for place in range(stages - 1):
            sent = g.fsdp_send(down_sums, place)
            down_sums = g.fsdp_add(down_sums, sent, place)
        branch_far, out_got, down_sums = lax.optimization_barrier((g.swap(branch_mine), out_got, down_sums))
        down_sent = g.fsdp_send(down_sums, stages - 1)
        branch_own = joined(branch_mine, branch_far)
        grad_mixed = matmul(branch_own, o_full).astype(LOW)
        o_part = outer(branch_own, mixed_own).astype(LOW)
        grad_att = g.exchange_pieces(
            lambda mask: lax.dynamic_slice_in_dim(grad_mixed, (g.c ^ mask) * q_cols, q_cols, 1)
        )
        grad_att = [grad_att[mask] for mask in g.order]
        grad_att, _, gu_sum, down_sent = lax.optimization_barrier((grad_att, o_part, gu_sum, down_sent))
        down_sums = g.fsdp_add(down_sums, down_sent, stages - 1)
        down_sum = jnp.concatenate([part[0].astype(LOW) for part in down_sums], axis=0)
        o_sum = sum_weight(o_part)
        gu_got = return_weight(gu_sum)
        grad_qkv = attention_back(query_rot, kv_rot, logs, grad_att, tables)
        qkv_part = outer(normed_one, grad_qkv).astype(LOW)
        grad_qkv, gu_got, o_sum, _ = lax.optimization_barrier((grad_qkv, gu_got, o_sum, qkv_part))
        o_got = return_weight(o_sum)
        qkv_sum = sum_weight(qkv_part)
        down_got = return_weight(down_sum)
        grad_own = jnp.concatenate(
            g.by_source(g.exchange_pieces(lambda mask: g.of_device(grad_qkv, mask))), axis=1
        )
        total = own_rows(g, grad_own, back_full)
        total, down_got, o_got = lax.optimization_barrier((total, down_got, o_got))
        out_total = out_keep + out_got.astype(WIDE)
        layer_output = g.both_halves((resid + out_total).astype(LOW))
        grad_normed_one = total

        gu_blocks = g.by_source(gu_got)
        gate_grad = cols(gu_blocks, 0, hid)
        up_grad = cols(gu_blocks, hid, hid)
        down_grad = cols(g.by_source(down_got), 0, hid)
        qkv_blocks = g.by_source(return_weight(qkv_sum))
        q_grad = cols(qkv_blocks, 0, q_cols)
        o_grad = sum(block.astype(WIDE) for block in o_got)

        def kv_grad(start):
            parts = [b[:, start : start + kv_cols].astype(WIDE) for b in qkv_blocks]
            copies = n_c * kv_cols // k_weight.shape[1]
            return jnp.concatenate([sum(parts[j : j + copies]) for j in range(0, n_c, copies)], axis=1)

        k_grad = kv_grad(q_cols)
        v_grad = kv_grad(q_cols + kv_cols)
        rms_mine = inverse_rms(x_mine)
        grad_in = grad_resid + norm_reverse(x_mine, rms_mine, gain_one, grad_normed_one)
        input_grad = g.both_halves(grad_in.astype(LOW))

        def gain_grad(gain, pairs):
            total = sum(jnp.sum(grad * weight.astype(LOW).astype(WIDE), axis=1) for grad, weight in pairs)
            return (total + g.swap(total)) / gain.astype(LOW).astype(WIDE)

        attn_gain_grad = gain_grad(attn_gain, [(q_grad, q_weight), (k_grad, k_weight), (v_grad, v_weight)])
        mlp_gain_grad = gain_grad(mlp_gain, [(gate_grad, gate_weight), (up_grad, up_weight)])
        return (
            layer_output[None],
            input_grad[None],
            attn_gain_grad,
            q_grad,
            k_grad,
            v_grad,
            o_grad,
            mlp_gain_grad,
            gate_grad,
            up_grad,
            down_grad,
        )

    return on_device


def solution(mesh):
    tokens = P("fsdp", "context", None)
    gain = P(("fsdp", "context"))
    weight = P(("fsdp", "context"), "tensor")
    return jax.shard_map(
        make_layer(mesh),
        mesh=mesh,
        in_specs=(tokens, P("fsdp"), gain, weight, weight, weight, weight, gain, weight, weight, weight, tokens),
        out_specs=(tokens, tokens, gain, weight, weight, weight, weight, gain, weight, weight, weight),
        check_vma=False,
    )
```
